32 devices in a mesh: gx: 4 (over y, x), gy: 2 (over core), gz: 4 (over z).
Axes of the slice: x: 2, y: 2, z: 4, core: 2. Of those that a mesh axis runs over, the one named last changes fastest.
Arguments:
- positions: float32 [3, 4, 4, 8, 128], P(None, 'gx', 'gy', 'gz'), may hold values from 0 to 1
- velocities: float32 [3, 4, 4, 8, 128], P(None, 'gx', 'gy', 'gz'), may hold values from -1.8 to 1.8
- species: int32 [4, 4, 8, 128], P('gx', 'gy', 'gz'), may hold values from 0 to 1
- counts: int32 [4, 4, 8], P('gx', 'gy', 'gz'), may hold values from 32 to 128
Outputs:
- new_positions: float32 [3, 4, 4, 8, 128], P(None, 'gx', 'gy', 'gz')
- new_velocities: float32 [3, 4, 4, 8, 128], P(None, 'gx', 'gy', 'gz')
The draws below stay inside these ranges and needn't reach their ends.
All inputs are finite; a program needn't handle non-finite values.
Results may differ from the reference program's by a relative error of at most 0.0003.
Values sent between devices are 32-bit elements; how exact they have to be, the bound alone decides.
No kernel may reach another device: no remote copies, remote signals or barrier semaphores. Data moves between devices by JAX's collectives and lax.ppermute only.
A program may use at most 64 MiB of HBM per device.

```python
from functools import partial
import jax
import jax.numpy as jnp
from jax import lax

SLOTS = 128
NCX = 4
NCY = 4
NCZ = 8


def plant(entries, stream_key, low, top_value):
    place = [jax.random.randint(jax.random.fold_in(stream_key, axis), (), 0, length) for axis, length in enumerate(entries.shape)]
    longest = entries.shape.index(max(entries.shape))
    neighbour = place[:longest] + [(place[longest] + 1) % entries.shape[longest]] + place[longest + 1:]
    return entries.at[tuple(place)].set(low).at[tuple(neighbour)].set(top_value)


def shard_levels(key, extent, shards, smallest, top_value):
    level = 1.0
    for dim, parts in shards:
        draws = jax.random.uniform(jax.random.fold_in(jax.random.fold_in(key, 6), dim), (parts,), jnp.float32, smallest / len(shards), top_value / len(shards))
        level = level * jnp.repeat(jnp.exp(draws), extent[dim] // parts).reshape((-1,) + (1,) * (len(extent) - 1 - dim))
    return level


def scatter_about(rng, dims, deviation, bound, pieces=(), kind=jnp.bfloat16):
    factor_of = shard_levels(rng, dims, pieces, -0.22, 0.18) if pieces else 1.0
    array = jax.random.normal(rng, dims, jnp.float32) * deviation * factor_of
    return jnp.minimum(jnp.maximum(array, -bound), bound).astype(kind)


def setup_inputs(seed: int = 0) -> dict:
    key_of = jax.random.split(jax.random.key(seed), 5)
    positions = jnp.clip(1.0 * jax.random.uniform(key_of[0], (3, NCX, NCY, NCZ, SLOTS), jnp.float32) ** shard_levels(key_of[0], (3, NCX, NCY, NCZ, SLOTS), ((1, 4), (2, 2), (3, 4)), -0.2, 0.2), 0.0, 1.0)
    velocities = scatter_about(key_of[1], (3, NCX, NCY, NCZ, SLOTS), 0.3, 1.8, ((1, 4), (2, 2), (3, 4)), jnp.float32)
    species = plant(jax.random.randint(key_of[2], (NCX, NCY, NCZ, SLOTS), 0, 2), jax.random.fold_in(key_of[2], 1), 0, 1).astype(jnp.int32)
    counts = plant(jax.random.randint(key_of[3], (NCX, NCY, NCZ), SLOTS // 4, SLOTS + 1), jax.random.fold_in(key_of[3], 1), SLOTS // 4, SLOTS).astype(jnp.int32)
    return {"positions": positions, "velocities": velocities, "species": species, "counts": counts}


time_step = 0.05
neighbour_offsets = [(first_step, second_step, third_step) for first_step in (-1, 0, 1) for second_step in (-1, 0, 1) for third_step in (-1, 0, 1)]

def coefficient(species, first, second):
    return jnp.where(species == 1, second, first).astype(jnp.float32)

def atom_records(species, counts):
    slot_index = lax.broadcasted_iota(jnp.int32, species.shape, 3)
    present = (slot_index < counts[..., None]).astype(jnp.float32)
    amplitude = coefficient(species, 1.0, 1.3) * present
    strength = coefficient(species, 0.3, 0.4) * present
    return (jnp.stack([amplitude, strength], axis=0), present)

def pair_geometry(owned, partner, offset):
    deltas = [partner[component][..., None, :] + float(offset[component]) - owned[component][..., :, None] for component in range(3)]
    square = deltas[0] * deltas[0] + deltas[1] * deltas[1] + deltas[2] * deltas[2]
    smooth = jnp.maximum(1.0 - square, 0.0)
    return (deltas, smooth)

def density_block(owned, partner, offset):
    deltas, smooth = pair_geometry(owned, partner, offset)
    contrib = partner[3][..., None, :] * smooth * smooth * smooth
    if offset == (0, 0, 0):
        slot_count = owned.shape[-1]
        contrib = contrib * (1.0 - jnp.eye(slot_count, dtype=jnp.float32))
    return lax.optimization_barrier(jnp.sum(contrib, axis=-1))

def force_block(owned, partner, slopes, partner_slopes, offset):
    deltas, smooth = pair_geometry(owned, partner, offset)
    weight = 3.0 * smooth * smooth * (slopes[..., :, None] * partner[3][..., None, :] + partner_slopes[..., None, :] * owned[3][..., :, None])
    weight = weight + 2.0 * owned[4][..., :, None] * partner[4][..., None, :] * smooth
    return jnp.stack([-2.0 * lax.optimization_barrier(jnp.sum(weight * deltas[component], axis=-1)) for component in range(3)], axis=0)

def plane_density(paired, offset):
    return density_block(paired[0], paired[1], offset)

def plane_force(paired, offset):
    return force_block(paired[0], paired[1], paired[2], paired[3], offset)

def density_field(atom_pack):
    density = jnp.zeros(atom_pack.shape[1:], jnp.float32)
    for offset in neighbour_offsets:
        partner = jnp.roll(atom_pack, (-offset[0], -offset[1], -offset[2]), axis=(1, 2, 3))
        portion = lax.map(partial(plane_density, offset=offset), (jnp.moveaxis(atom_pack, 1, 0), jnp.moveaxis(partner, 1, 0)))
        density = density + portion
    return density

def force_field(atom_pack, slopes):
    forces = jnp.zeros((3,) + atom_pack.shape[1:], jnp.float32)
    for offset in neighbour_offsets:
        partner = jnp.roll(atom_pack, (-offset[0], -offset[1], -offset[2]), axis=(1, 2, 3))
        partner_slopes = jnp.roll(slopes, (-offset[0], -offset[1], -offset[2]), axis=(0, 1, 2))
        portion = lax.map(partial(plane_force, offset=offset), (jnp.moveaxis(atom_pack, 1, 0), jnp.moveaxis(partner, 1, 0), slopes, partner_slopes))
        forces = forces + jnp.moveaxis(portion, 0, 1)
    return forces

def reference(positions, velocities, species, counts):
    records, present = atom_records(species, counts)
    inverse_mass = coefficient(species, 1.0, 1.6)

    def compute_forces(location):
        atom_pack = jnp.concatenate([location, records], axis=0)
        density = density_field(atom_pack)
        slopes = -0.5 * present / jnp.sqrt(density + 1.0)
        return force_field(atom_pack, slopes)
    location = positions
    velocity = velocities
    forces = compute_forces(location)
    for sweep in range(2):
        velocity = velocity + 0.5 * time_step * inverse_mass * forces
        location = location + time_step * velocity
        forces = compute_forces(location)
        velocity = velocity + 0.5 * time_step * inverse_mass * forces
    return (location, velocity)
```

```python
import functools

import jax
import jax.numpy as jnp
from jax import lax
from jax.experimental import pallas as pl
from jax.experimental.pallas import tpu as pltpu
from jax.sharding import PartitionSpec as P

time_step = 0.05
half_kick = 0.5 * time_step
LANES = 128
ROOT = 1.3 ** (1.0 / 3.0)


def ring_halo(cells, axis, dim, width):
    count = lax.axis_size(axis)
    size = cells.shape[dim]
    head = lax.slice_in_dim(cells, 0, width, axis=dim)
    tail = lax.slice_in_dim(cells, size - width, size, axis=dim)
    if count == 1:
        return jnp.concatenate([tail, cells, head], axis=dim)
    if count == 2 and size == 2 * width:
        other = lax.ppermute(cells, axis, [(0, 1), (1, 0)])
        return jnp.concatenate(
            [
                lax.slice_in_dim(other, width, size, axis=dim),
                cells,
                lax.slice_in_dim(other, 0, width, axis=dim),
            ],
            axis=dim,
        )
    below = lax.ppermute(tail, axis, [(i, (i + 1) % count) for i in range(count)])
    above = lax.ppermute(head, axis, [((i + 1) % count, i) for i in range(count)])
    return jnp.concatenate([below, cells, above], axis=dim)


def by_code(code, first, second):
    return jnp.where(code > 1.5, second, jnp.where(code > 0.5, first, 0.0))


def split3(value):
    high = value.astype(jnp.bfloat16).astype(jnp.float32)
    rest = value - high
    middle = rest.astype(jnp.bfloat16).astype(jnp.float32)
    return high, middle, rest - middle


def row_masks():
    row = lax.broadcasted_iota(jnp.int32, (8, LANES), 0)
    masks = [(row == k).astype(jnp.float32) for k in range(5)]
    return masks, masks[0] + masks[1] + masks[2]


def placed(tile, centre, masks, spatial):
    point = tile * spatial
    for axis in range(3):
        if centre[axis]:
            point = point + centre[axis] * masks[axis]
    return point, jnp.sum(point * point, axis=0, keepdims=True)


def partner_features(tile, centre, masks, spatial):
    point, norm = placed(tile, centre, masks, spatial)
    scale = by_code(tile[3:4], 1.0, ROOT)
    row = (point - norm * masks[3] + masks[4]) * scale
    high, middle, low = split3(row)
    first = jnp.concatenate([high, middle], axis=0).astype(jnp.bfloat16)
    last = jnp.concatenate([low, high], axis=0).astype(jnp.bfloat16)
    return point, jnp.concatenate([first, first, last], axis=0)


def target_features(tile, centre, masks, spatial):
    point, norm = placed(tile, centre, masks, spatial)
    high, middle, low = split3(2.0 * point + masks[3] + (1.0 - norm) * masks[4])
    stacked = jnp.concatenate([high, high, middle, middle, high, low], axis=0)
    return point, jnp.transpose(stacked).astype(jnp.bfloat16)


def centre_of(cell, extent):
    return tuple(float(c) - 0.5 * e for c, e in zip(cell, extent))


def density_kernel(extent, feat_ref, slope_ref, part_ref):
    ex, ey, ez = extent
    masks, spatial = row_masks()
    for a in range(ex):
        for b in range(ey):
            for c in range(ez):
                index = (a * ey + b) * ez + c
                _, block = partner_features(
                    feat_ref[index], centre_of((a, b, c), extent), masks, spatial
                )
                part_ref[:, index * LANES : (index + 1) * LANES] = block
    place = 0
    rows = 64
    for a in range(1, ex - 1):
        for b in range(1, ey - 1):
            for c in range(1, ez - 1):
                index = (a * ey + b) * ez + c
                tile = feat_ref[index]
                _, left = target_features(tile, centre_of((a, b, c), extent), masks, spatial)
                sums = []
                for start in range(0, LANES, rows):
                    total = jnp.zeros((rows, LANES), jnp.float32)
                    for p in (-1, 0, 1):
                        for q in (-1, 0, 1):
                            base = ((a + p) * ey + b + q) * ez + c - 1
                            near = jnp.dot(
                                left[start : start + rows],
                                part_ref[:, base * LANES : (base + 3) * LANES],
                                preferred_element_type=jnp.float32,
                            )
                            for k in range(3):
                                part = jnp.maximum(near[:, k * LANES : (k + 1) * LANES], 0.0)
                                if p == 0 and q == 0 and k == 1:
                                    i = lax.broadcasted_iota(jnp.int32, (rows, LANES), 0)
                                    j = lax.broadcasted_iota(jnp.int32, (rows, LANES), 1)
                                    part = jnp.where(i + start == j, 0.0, part)
                                total = total + part * part * part
                    sums.append(total)
                density = jnp.sum(jnp.transpose(jnp.concatenate(sums, axis=0)), axis=0, keepdims=True)
                present = by_code(tile[3:4], 1.0, 1.0)
                slope_ref[place : place + 1, :] = -0.5 * present / jnp.sqrt(density + 1.0)
                place += 1


def force_kernel(extent, stage, feat_ref, slope_ref, vel_ref, *refs):
    if stage == "last":
        new_vel_ref, part_ref, value_ref = refs
    else:
        new_vel_ref, new_loc_ref, part_ref, value_ref = refs
    ex, ey, ez = extent
    near_z = ez - 2
    masks, spatial = row_masks()
    for a in range(ex):
        for b in range(ey):
            for c in range(near_z):
                index = (a * ey + b) * near_z + c
                tile = feat_ref[(a * ey + b) * ez + c + 1]
                point, block = partner_features(
                    tile, centre_of((a, b, c + 1), extent), masks, spatial
                )
                lanes = slice(index * LANES, (index + 1) * LANES)
                part_ref[:, lanes] = block
                code = tile[3:4]
                slope = slope_ref[index : index + 1, :]
                value_ref[:, lanes] = (
                    point
                    + by_code(code, 3.0, 3.0 * ROOT) * masks[3]
                    + (slope * by_code(code, 3.0, 3.0 / (ROOT * ROOT))) * masks[4]
                )
                value_ref[5:6, lanes] = by_code(code, 0.6, 0.8 / ROOT)
    place = 0
    rows = 32
    for a in range(1, ex - 1):
        for b in range(1, ey - 1):
            for c in range(2, ez - 2):
                tile = feat_ref[(a * ey + b) * ez + c]
                point, left = target_features(tile, centre_of((a, b, c), extent), masks, spatial)
                code = tile[3:4]
                index = (a * ey + b) * near_z + c - 1
                slope = slope_ref[index : index + 1, :]
                solute = code > 1.5
                u = slope * jnp.where(solute, 1.0 / 1.3, 1.0)
                rho = jnp.where(solute, 0.4 / 1.3, 0.3)
                columns = jnp.transpose(u * masks[0] + rho * masks[1])
                sums = [[] for _ in range(4)]
                for start in range(0, LANES, rows):
                    u_i = jnp.broadcast_to(columns[start : start + rows, 0:1], (rows, LANES))
                    rho_i = jnp.broadcast_to(columns[start : start + rows, 1:2], (rows, LANES))
                    total = [jnp.zeros((rows, LANES), jnp.float32) for _ in range(4)]
                    for p in (-1, 0, 1):
                        for q in (-1, 0, 1):
                            base = ((a + p) * ey + b + q) * near_z + c - 2
                            near = jnp.dot(
                                left[start : start + rows],
                                part_ref[:, base * LANES : (base + 3) * LANES],
                                preferred_element_type=jnp.float32,
                            )
                            for k in range(3):
                                lanes = slice((base + k) * LANES, (base + k + 1) * LANES)
                                s = jnp.maximum(near[:, k * LANES : (k + 1) * LANES], 0.0)
                                w = u_i * value_ref[3:4, lanes] + value_ref[4:5, lanes]
                                w = (w * s + rho_i * value_ref[5:6, lanes]) * s
                                total[3] = total[3] + w
                                for axis in range(3):
                                    total[axis] = total[axis] + w * value_ref[axis : axis + 1, lanes]
                    for k in range(4):
                        sums[k].append(total[k])
                flat = [
                    jnp.sum(jnp.transpose(jnp.concatenate(parts, axis=0)), axis=0, keepdims=True)
                    for parts in sums
                ]
                amplitude = by_code(code, 1.0, 1.3)
                kick = half_kick * jnp.where(solute, 1.6, 1.0)
                for axis in range(3):
                    force = -2.0 * amplitude * (flat[axis] - point[axis : axis + 1] * flat[3])
                    speed = vel_ref[place, axis : axis + 1, :] + kick * force
                    if stage == "middle":
                        speed = speed + kick * force
                    new_vel_ref[place, axis : axis + 1, :] = speed
                    if stage != "last":
                        new_loc_ref[place, axis : axis + 1, :] = (
                            tile[axis : axis + 1] + time_step * speed
                        )
                if stage != "last":
                    new_loc_ref[place, 3:4, :] = code
                place += 1


def on_device(positions, velocities, species, counts):
    cx, cy, cz, slots = positions.shape[1:]
    present = lax.broadcasted_iota(jnp.int32, species.shape, 3) < counts[..., None]
    code = jnp.where(present, jnp.where(species == 1, 2.0, 1.0), 0.0)
    location = jnp.concatenate([jnp.moveaxis(positions, 0, 3), code[..., None, :]], axis=3)
    velocity = jnp.moveaxis(velocities, 0, 3).reshape(cx * cy * cz, 3, slots)
    extent = (cx + 2, cy + 2, cz + 4)
    own = cx * cy * cz
    cells = extent[0] * extent[1] * extent[2]
    near = extent[0] * extent[1] * (cz + 2)
    vmem = pl.BlockSpec(memory_space=pltpu.VMEM)

    def evaluate(location, velocity, stage):
        wide = ring_halo(location, "gy", 1, 1)
        wide = ring_halo(wide, "gx", 0, 1)
        wide = ring_halo(wide, "gz", 2, 2)
        feat = jnp.pad(wide.reshape(cells, 4, slots), ((0, 0), (0, 4), (0, 0)))
        slopes = pl.pallas_call(
            functools.partial(density_kernel, extent),
            out_shape=jax.ShapeDtypeStruct((cx * cy * (cz + 2), slots), jnp.float32),
            in_specs=[vmem],
            out_specs=vmem,
            scratch_shapes=[pltpu.VMEM((48, cells * slots), jnp.bfloat16)],
            name="density",
        )(feat)
        slopes = slopes.reshape(cx, cy, cz + 2, slots)
        slopes = ring_halo(slopes, "gy", 1, 1)
        slopes = ring_halo(slopes, "gx", 0, 1).reshape(near, slots)
        out_shape = [jax.ShapeDtypeStruct((own, 3, slots), jnp.float32)]
        if stage != "last":
            out_shape.append(jax.ShapeDtypeStruct((own, 4, slots), jnp.float32))
        out = pl.pallas_call(
            functools.partial(force_kernel, extent, stage),
            out_shape=out_shape,
            in_specs=[vmem] * 3,
            out_specs=[vmem] * len(out_shape),
            scratch_shapes=[
                pltpu.VMEM((48, near * slots), jnp.bfloat16),
                pltpu.VMEM((8, near * slots), jnp.float32),
            ],
            name="force_" + stage,
        )(feat, slopes, velocity)
        if stage == "last":
            return location, out[0]
        return out[1].reshape(location.shape), out[0]

    location, velocity = evaluate(location, velocity, "first")
    location, velocity = evaluate(location, velocity, "middle")
    location, velocity = evaluate(location, velocity, "last")
    new_positions = jnp.moveaxis(location[..., :3, :], 3, 0)
    new_velocities = jnp.moveaxis(velocity.reshape(cx, cy, cz, 3, slots), 3, 0)
    return new_positions, new_velocities


def solution(mesh):
    return jax.shard_map(
        on_device,
        mesh=mesh,
        in_specs=(
            P(None, "gx", "gy", "gz", None),
            P(None, "gx", "gy", "gz", None),
            P("gx", "gy", "gz", None),
            P("gx", "gy", "gz"),
        ),
        out_specs=(P(None, "gx", "gy", "gz", None), P(None, "gx", "gy", "gz", None)),
        check_vma=False,
    )
```

```python
import functools

import jax
import jax.numpy as jnp
from jax import lax
from jax.experimental import pallas as pl
from jax.experimental.pallas import tpu as pltpu
from jax.sharding import PartitionSpec as P

time_step = 0.05
half_kick = 0.5 * time_step
LANES = 128
GRANT = 8 * 1024 * 1024
ROOT = 1.3 ** (1.0 / 3.0)


def ring_halo(cells, axis, dim, width):
    count = lax.axis_size(axis)
    size = cells.shape[dim]
    head = lax.slice_in_dim(cells, 0, width, axis=dim)
    tail = lax.slice_in_dim(cells, size - width, size, axis=dim)
    if count == 1:
        return jnp.concatenate([tail, cells, head], axis=dim)
    if count == 2 and size == 2 * width:
        other = lax.ppermute(cells, axis, [(0, 1), (1, 0)])
        return jnp.concatenate(
            [
                lax.slice_in_dim(other, width, size, axis=dim),
                cells,
                lax.slice_in_dim(other, 0, width, axis=dim),
            ],
            axis=dim,
        )
    below = lax.ppermute(tail, axis, [(i, (i + 1) % count) for i in range(count)])
    above = lax.ppermute(head, axis, [((i + 1) % count, i) for i in range(count)])
    return jnp.concatenate([below, cells, above], axis=dim)


def by_code(code, first, second):
    return jnp.where(code > 1.5, second, jnp.where(code > 0.5, first, 0.0))


def split3(value):
    high = value.astype(jnp.bfloat16).astype(jnp.float32)
    rest = value - high
    middle = rest.astype(jnp.bfloat16).astype(jnp.float32)
    return high, middle, rest - middle


def row_masks():
    row = lax.broadcasted_iota(jnp.int32, (8, LANES), 0)
    masks = [(row == k).astype(jnp.float32) for k in range(7)]
    return masks, masks[0] + masks[1] + masks[2]


def placed(tile, centre, masks, spatial):
    point = tile * spatial
    for axis in range(3):
        if centre[axis]:
            point = point + centre[axis] * masks[axis]
    return point, jnp.sum(point * point, axis=0, keepdims=True)


def partner_block(row):
    high, middle, low = split3(row)
    first = jnp.concatenate([high, middle], axis=0).astype(jnp.bfloat16)
    last = jnp.concatenate([low, high], axis=0).astype(jnp.bfloat16)
    return jnp.concatenate([first, first, last], axis=0)


def target_block(row):
    high, middle, low = split3(row)
    stacked = jnp.concatenate([high, high, middle, middle, high, low], axis=0)
    return jnp.transpose(stacked).astype(jnp.bfloat16)


def centre_of(cell, extent):
    return tuple(float(c) - 0.5 * e for c, e in zip(cell, extent))


def density_kernel(extent, feat_ref, slope_ref, part_ref):
    ex, ey, ez = extent
    masks, spatial = row_masks()
    for a in range(ex):
        for b in range(ey):
            for c in range(ez):
                index = (a * ey + b) * ez + c
                tile = feat_ref[index]
                point, norm = placed(tile, centre_of((a, b, c), extent), masks, spatial)
                scale = by_code(tile[3:4], 1.0, ROOT)
                part_ref[:, index * LANES : (index + 1) * LANES] = partner_block(
                    (point - norm * masks[3] + masks[4]) * scale
                )
    place = 0
    rows = 64
    for a in range(1, ex - 1):
        for b in range(1, ey - 1):
            for c in range(1, ez - 1):
                index = (a * ey + b) * ez + c
                tile = feat_ref[index]
                point, norm = placed(tile, centre_of((a, b, c), extent), masks, spatial)
                left = target_block(2.0 * point + masks[3] + (1.0 - norm) * masks[4])
                sums = []
                for start in range(0, LANES, rows):
                    total = jnp.zeros((rows, LANES), jnp.float32)
                    for p in (-1, 0, 1):
                        for q in (-1, 0, 1):
                            base = ((a + p) * ey + b + q) * ez + c - 1
                            near = jnp.dot(
                                left[start : start + rows],
                                part_ref[:, base * LANES : (base + 3) * LANES],
                                preferred_element_type=jnp.float32,
                            )
                            for k in range(3):
                                part = jnp.maximum(near[:, k * LANES : (k + 1) * LANES], 0.0)
                                if p == 0 and q == 0 and k == 1:
                                    i = lax.broadcasted_iota(jnp.int32, (rows, LANES), 0)
                                    j = lax.broadcasted_iota(jnp.int32, (rows, LANES), 1)
                                    part = jnp.where(i + start == j, 0.0, part)
                                total = total + part * part * part
                    sums.append(total)
                density = jnp.sum(jnp.transpose(jnp.concatenate(sums, axis=0)), axis=0, keepdims=True)
                present = by_code(tile[3:4], 1.0, 1.0)
                slope_ref[place : place + 1, :] = -0.5 * present / jnp.sqrt(density + 1.0)
                place += 1


def force_kernel(extent, stage, feat_ref, slope_ref, vel_ref, *refs):
    if stage == "first":
        new_vel_ref, new_loc_ref, part_ref, pair_ref, point_ref = refs
    elif stage == "middle":
        new_vel_ref, new_loc_ref, new_pos_ref, part_ref, pair_ref, point_ref = refs
    else:
        new_vel_ref, part_ref, pair_ref, point_ref = refs
    ex, ey, ez = extent
    near_z = ez - 2
    masks, spatial = row_masks()
    for a in range(ex):
        for b in range(ey):
            for c in range(near_z):
                index = (a * ey + b) * near_z + c
                lanes = slice(index * LANES, (index + 1) * LANES)
                tile = feat_ref[(a * ey + b) * ez + c + 1]
                point, norm = placed(tile, centre_of((a, b, c + 1), extent), masks, spatial)
                code = tile[3:4]
                scale = by_code(code, 0.6, 0.8)
                part_ref[:, lanes] = partner_block(
                    (point - norm * masks[3] + masks[4]) * scale
                )
                slope = slope_ref[index : index + 1, :]
                pair_ref[:, lanes] = partner_block(
                    by_code(code, 0.75 / 0.09, 0.75 * 1.3 / 0.16) * masks[5]
                    + slope * by_code(code, 0.75 / 0.09, 0.75 / 0.16) * masks[6]
                )
                point_ref[:, lanes] = point
    place = 0
    rows = 32
    for a in range(1, ex - 1):
        for b in range(1, ey - 1):
            for c in range(2, ez - 2):
                tile = feat_ref[(a * ey + b) * ez + c]
                point, norm = placed(tile, centre_of((a, b, c), extent), masks, spatial)
                code = tile[3:4]
                solute = code > 1.5
                index = (a * ey + b) * near_z + c - 1
                slope = slope_ref[index : index + 1, :]
                strength = jnp.where(solute, 0.4, 0.3)
                left = target_block(
                    (2.0 * point + masks[3] + (1.0 - norm) * masks[4]) * strength
                    + slope * jnp.where(solute, 1.0 / 0.16, 1.0 / 0.09) * masks[5]
                    + jnp.where(solute, 1.3 / 0.16, 1.0 / 0.09) * masks[6]
                )
                sums = [[] for _ in range(4)]
                for start in range(0, LANES, rows):
                    total = [jnp.zeros((rows, LANES), jnp.float32) for _ in range(4)]
                    for p in (-1, 0, 1):
                        for q in (-1, 0, 1):
                            base = ((a + p) * ey + b + q) * near_z + c - 2
                            span = slice(base * LANES, (base + 3) * LANES)
                            near = jnp.dot(
                                left[start : start + rows],
                                part_ref[:, span],
                                preferred_element_type=jnp.float32,
                            )
                            kappa = jnp.dot(
                                left[start : start + rows],
                                pair_ref[:, span],
                                preferred_element_type=jnp.float32,
                            )
                            for k in range(3):
                                lanes = slice((base + k) * LANES, (base + k + 1) * LANES)
                                s = jnp.maximum(near[:, k * LANES : (k + 1) * LANES], 0.0)
                                w = s * (1.0 + s * kappa[:, k * LANES : (k + 1) * LANES])
                                total[3] = total[3] + w
                                for axis in range(3):
                                    total[axis] = total[axis] + w * point_ref[axis : axis + 1, lanes]
                    for k in range(4):
                        sums[k].append(total[k])
                flat = [
                    jnp.sum(jnp.transpose(jnp.concatenate(parts, axis=0)), axis=0, keepdims=True)
                    for parts in sums
                ]
                present = by_code(code, 1.0, 1.0)
                kick = half_kick * jnp.where(solute, 1.6, 1.0)
                row = slice(place, place + 1)
                for axis in range(3):
                    force = -2.0 * present * (flat[axis] - point[axis : axis + 1] * flat[3])
                    speed = vel_ref[axis, row, :] + kick * force
                    if stage == "middle":
                        speed = speed + kick * force
                    new_vel_ref[axis, row, :] = speed
                    if stage != "last":
                        moved = tile[axis : axis + 1] + time_step * speed
                        new_loc_ref[place, axis : axis + 1, :] = moved
                        if stage == "middle":
                            new_pos_ref[axis, row, :] = moved
                if stage != "last":
                    new_loc_ref[place, 3:4, :] = code
                place += 1


def on_device(positions, velocities, species, counts):
    cx, cy, cz, slots = positions.shape[1:]
    present = lax.broadcasted_iota(jnp.int32, species.shape, 3) < counts[..., None]
    code = jnp.where(present, jnp.where(species == 1, 2.0, 1.0), 0.0)
    location = jnp.concatenate([jnp.moveaxis(positions, 0, 3), code[..., None, :]], axis=3)
    extent = (cx + 2, cy + 2, cz + 4)
    own = cx * cy * cz
    cells = extent[0] * extent[1] * extent[2]
    near = extent[0] * extent[1] * (cz + 2)
    velocity = velocities.reshape(3, own, slots)
    vmem = pl.BlockSpec(memory_space=pltpu.VMEM)
    flat_shape = jax.ShapeDtypeStruct((3, own, slots), jnp.float32)

    def evaluate(location, velocity, stage):
        wide = ring_halo(location, "gy", 1, 1)
        wide = ring_halo(wide, "gx", 0, 1)
        wide = ring_halo(wide, "gz", 2, 2)
        feat = jnp.pad(wide.reshape(cells, 4, slots), ((0, 0), (0, 4), (0, 0)))
        slopes = pl.pallas_call(
            functools.partial(density_kernel, extent),
            out_shape=jax.ShapeDtypeStruct((cx * cy * (cz + 2), slots), jnp.float32),
            in_specs=[vmem],
            out_specs=vmem,
            scratch_shapes=[pltpu.VMEM((48, cells * slots), jnp.bfloat16)],
            compiler_params=pltpu.CompilerParams(vmem_limit_bytes=GRANT),
            name="density",
        )(feat)
        slopes = slopes.reshape(cx, cy, cz + 2, slots)
        slopes = ring_halo(slopes, "gy", 1, 1)
        slopes = ring_halo(slopes, "gx", 0, 1).reshape(near, slots)
        out_shape = [flat_shape]
        if stage != "last":
            out_shape.append(jax.ShapeDtypeStruct((own, 4, slots), jnp.float32))
        if stage == "middle":
            out_shape.append(flat_shape)
        return pl.pallas_call(
            functools.partial(force_kernel, extent, stage),
            out_shape=out_shape,
            in_specs=[vmem] * 3,
            out_specs=[vmem] * len(out_shape),
            scratch_shapes=[
                pltpu.VMEM((48, near * slots), jnp.bfloat16),
                pltpu.VMEM((48, near * slots), jnp.bfloat16),
                pltpu.VMEM((8, near * slots), jnp.float32),
            ],
            compiler_params=pltpu.CompilerParams(vmem_limit_bytes=GRANT),
            name="force_" + stage,
        )(feat, slopes, velocity)

    velocity, moved = evaluate(location, velocity, "first")
    velocity, moved, new_positions = evaluate(moved.reshape(location.shape), velocity, "middle")
    (velocity,) = evaluate(moved.reshape(location.shape), velocity, "last")
    return new_positions.reshape(positions.shape), velocity.reshape(positions.shape)


def solution(mesh):
    return jax.shard_map(
        on_device,
        mesh=mesh,
        in_specs=(
            P(None, "gx", "gy", "gz", None),
            P(None, "gx", "gy", "gz", None),
            P("gx", "gy", "gz", None),
            P("gx", "gy", "gz"),
        ),
        out_specs=(P(None, "gx", "gy", "gz", None), P(None, "gx", "gy", "gz", None)),
        check_vma=False,
    )
```

```python
import functools

import jax
import jax.numpy as jnp
from jax import lax
from jax.experimental import pallas as pl
from jax.experimental.pallas import tpu as pltpu
from jax.sharding import PartitionSpec as P

time_step = 0.05
half_kick = 0.5 * time_step
LANES = 128
GRANT = 8 * 1024 * 1024
ROOT = 1.3 ** (1.0 / 3.0)
STEPS = (-1, 0, 1)


def neighbours(cells, axis, dim, width):
    count = lax.axis_size(axis)
    size = cells.shape[dim]
    head = lax.slice_in_dim(cells, 0, width, axis=dim)
    tail = lax.slice_in_dim(cells, size - width, size, axis=dim)
    if count == 1:
        return tail, head
    if count == 2 and size == 2 * width:
        other = lax.ppermute(cells, axis, [(0, 1), (1, 0)])
        return (
            lax.slice_in_dim(other, width, size, axis=dim),
            lax.slice_in_dim(other, 0, width, axis=dim),
        )
    below = lax.ppermute(tail, axis, [(i, (i + 1) % count) for i in range(count)])
    above = lax.ppermute(head, axis, [((i + 1) % count, i) for i in range(count)])
    return below, above


def ring_halo(cells, axis, dim, width):
    below, above = neighbours(cells, axis, dim, width)
    return jnp.concatenate([below, cells, above], axis=dim)


def split3(value):
    high = value.astype(jnp.bfloat16).astype(jnp.float32)
    rest = value - high
    middle = rest.astype(jnp.bfloat16).astype(jnp.float32)
    return high, middle, rest - middle


def partner_block(row):
    high, middle, low = split3(row)
    first = jnp.concatenate([high, middle], axis=0).astype(jnp.bfloat16)
    last = jnp.concatenate([low, high], axis=0).astype(jnp.bfloat16)
    return jnp.concatenate([first, first, last], axis=0)


def target_block(row):
    high, middle, low = split3(row)
    stacked = jnp.concatenate([high, high, middle, middle, high, low], axis=0)
    return jnp.transpose(stacked).astype(jnp.bfloat16)


class Grid:
    def __init__(self, own):
        self.own = own
        self.ex, self.ey, self.ez = own[0] + 2, own[1] + 2, own[2] + 4
        self.plane = self.ex * self.ey
        row = lax.broadcasted_iota(jnp.int32, (8, LANES), 0)
        self.row = row
        self.masks = [(row == k).astype(jnp.float32) for k in range(7)]
        self.spatial = self.masks[0] + self.masks[1] + self.masks[2]

    def lanes(self, a, b, layer, count=1):
        base = ((layer * self.ex + a) * self.ey + b) * LANES
        return slice(base, base + count * LANES)

    def placed(self, tile, a, b, c):
        m = self.masks
        shift = (
            (a + 0.5 - 0.5 * self.ex) * m[0]
            + (b + 0.5 - 0.5 * self.ey) * m[1]
            + (m[4] + (c + 0.5 - 0.5 * self.ez) * m[2])
        )
        point = jnp.concatenate([tile, jnp.zeros((4, LANES), jnp.float32)], axis=0)
        point = point * self.spatial + shift
        return point, jnp.sum(point * point, axis=0, keepdims=True)

    def partner(self, tile, a, b, c):
        point, bulk = self.placed(tile, a, b, c)
        scale = tile[3:4]
        block = partner_block(jnp.where(self.row == 3, 1.0 - bulk, point) * scale)
        strength = jnp.where(scale > 1.05, 0.4 / ROOT, 0.3)
        return block, jnp.where(self.row == 3, strength, point)

    def target(self, tile, a, b, c):
        point, bulk = self.placed(tile, a, b, c)
        twice = jnp.where(self.row == 4, 2.0 - bulk, 2.0 * point)
        return point, twice + self.masks[3]


def density_of(grid, left, a, b, sources, skip):
    rows = 64
    sums = []
    for start in range(0, LANES, rows):
        total = jnp.zeros((rows, LANES), jnp.float32)
        for ref, layer, same in sources:
            for p in STEPS:
                near = jnp.dot(
                    left[start : start + rows],
                    ref[:, grid.lanes(a + p, b - 1, layer, 3)],
                    preferred_element_type=jnp.float32,
                )
                for k in range(3):
                    part = jnp.maximum(near[:, k * LANES : (k + 1) * LANES], 0.0)
                    if same and p == 0 and k == 1:
                        i = lax.broadcasted_iota(jnp.int32, (rows, LANES), 0)
                        j = lax.broadcasted_iota(jnp.int32, (rows, LANES), 1)
                        part = jnp.where(i + start == j, 0.0, part)
                    total = total + part * part * part
        sums.append(total)
    return jnp.sum(jnp.transpose(jnp.concatenate(sums, axis=0)), axis=0, keepdims=True)


def own_cells(own):
    return [(a, b, c) for a in range(1, own[0] + 1) for b in range(1, own[1] + 1) for c in range(own[2])]


def inner_density_kernel(own, mid_ref, sum_ref, part_ref, point_ref):
    grid = Grid(own)
    for c in range(own[2]):
        for a in range(grid.ex):
            for b in range(grid.ey):
                lanes = grid.lanes(a, b, c)
                part_ref[:, lanes], point_ref[:, lanes] = grid.partner(mid_ref[a, b, c], a, b, c + 2)
    for place, (a, b, c) in enumerate(own_cells(own)):
        _, row = grid.target(mid_ref[a, b, c], a, b, c + 2)
        layers = [c + r for r in STEPS if 0 <= c + r < own[2]]
        sources = [(part_ref, layer, layer == c) for layer in layers]
        sum_ref[place : place + 1, :] = density_of(grid, target_block(row), a, b, sources, c)


def outer_density_kernel(own, mid_ref, low_ref, high_ref, sum_ref, part_ref, slope_ref, edge_ref, edge_point_ref, far_ref):
    grid = Grid(own)
    cz = own[2]
    for ref, layer, where, c in ((low_ref, 0, 0, 0), (low_ref, 1, 0, 1), (high_ref, 0, 1, cz + 2), (high_ref, 1, 1, cz + 3)):
        edge = c in (1, cz + 2)
        for a in range(grid.ex):
            for b in range(grid.ey):
                lanes = grid.lanes(a, b, where)
                block, point = grid.partner(ref[a, b, layer], a, b, c)
                if edge:
                    edge_ref[:, lanes] = block
                    edge_point_ref[:, lanes] = point
                else:
                    far_ref[:, lanes] = block

    def finish(place, tile, density):
        present = jnp.where(tile[3:4] > 0.5, -0.5, 0.0)
        slope_ref[place : place + 1, :] = present / jnp.sqrt(density + 1.0)

    for a in range(1, own[0] + 1):
        for b in range(1, own[1] + 1):
            first = ((a - 1) * own[1] + b - 1) * (cz + 2)
            for side in (0, 1):
                tile = (low_ref[a, b, 1], high_ref[a, b, 0])[side]
                c = (1, cz + 2)[side]
                _, row = grid.target(tile, a, b, c)
                sources = [(far_ref, side, False), (edge_ref, side, True), (part_ref, (0, cz - 1)[side], False)]
                finish(first + side * (cz + 1), tile, density_of(grid, target_block(row), a, b, sources, c))
            for c in range(cz):
                tile = mid_ref[a, b, c]
                place = ((a - 1) * own[1] + b - 1) * cz + c
                density = sum_ref[place : place + 1, :]
                sources = [(edge_ref, side, False) for side in (0, 1) if c == (0, cz - 1)[side]]
                if sources:
                    _, row = grid.target(tile, a, b, c + 2)
                    density = density + density_of(grid, target_block(row), a, b, sources, c)
                finish(first + 1 + c, tile, density)


def pair_block(grid, scale, slope):
    inverse = jnp.where(scale > 1.05, 0.75 / (ROOT * ROOT), 0.75)
    row = jnp.where(grid.row == 5, 0.75 * scale, jnp.where(grid.row == 6, slope * inverse, 0.0))
    return partner_block(row)


def force_sums(grid, own, spread, mid_ref, slope, part_ref, point_ref, edge_ref, edge_point_ref, pair_ref, place):
    rows = 32
    cz = own[2]
    a, b, c = place
    tile = mid_ref[a, b, c]
    point, row = grid.target(tile, a, b, c + 2)
    solute = tile[3:4] > 1.05
    m = grid.masks
    left = target_block(
        row * jnp.where(solute, 0.8, 0.6)
        + slope(a, b, c + 1) * jnp.where(solute, 1.0 / 0.16, 1.0 / 0.09) * m[5]
        + jnp.where(solute, 1.3 / 0.16, 1.0 / 0.09) * m[6]
    )
    sums = [[] for _ in range(4)]
    for start in range(0, LANES, rows):
        total = [jnp.zeros((rows, LANES), jnp.float32) for _ in range(4)]
        for r in STEPS:
            inner = 0 <= c + r < cz
            ref, value_ref, layer = (
                (part_ref, point_ref, c + r) if inner else (edge_ref, edge_point_ref, int(c + r >= cz))
            )
            for p in spread:
                near = jnp.dot(
                    left[start : start + rows],
                    ref[:, grid.lanes(a + p, b - 1, layer, 3)],
                    preferred_element_type=jnp.float32,
                )
                kappa = jnp.dot(
                    left[start : start + rows],
                    pair_ref[:, grid.lanes(a + p, b - 1, c + r + 1, 3)],
                    preferred_element_type=jnp.float32,
                )
                for k in range(3):
                    lanes = grid.lanes(a + p, b - 1 + k, layer)
                    s = jnp.maximum(near[:, k * LANES : (k + 1) * LANES], 0.0)
                    w = s * (value_ref[3:4, lanes] + s * kappa[:, k * LANES : (k + 1) * LANES])
                    total[3] = total[3] + w
                    for axis in range(3):
                        total[axis] = total[axis] + w * value_ref[axis : axis + 1, lanes]
        for k in range(4):
            sums[k].append(total[k])
    flat = [
        jnp.sum(jnp.transpose(jnp.concatenate(parts, axis=0)), axis=0, keepdims=True) for parts in sums
    ]
    return point, flat


def scale_of(own, mid_ref, low_ref, high_ref, a, b, near):
    if near == 0:
        return low_ref[a, b, 1][3:4]
    if near == own[2] + 1:
        return high_ref[a, b, 0][3:4]
    return mid_ref[a, b, near - 1][3:4]


def column_force_kernel(own, mid_ref, low_ref, high_ref, slope_ref, part_ref, point_ref, edge_ref, edge_point_ref, out_ref, pair_ref):
    grid = Grid(own)

    def slope(a, b, near):
        index = ((a - 1) * grid.ey + b) * (own[2] + 2) + near
        return slope_ref[index : index + 1, :]

    for near in range(own[2] + 2):
        for a in range(1, own[0] + 1):
            for b in range(grid.ey):
                scale = scale_of(own, mid_ref, low_ref, high_ref, a, b, near)
                pair_ref[:, grid.lanes(a, b, near)] = pair_block(grid, scale, slope(a, b, near))
    for place, cell in enumerate(own_cells(own)):
        _, flat = force_sums(
            grid, own, (0,), mid_ref, slope, part_ref, point_ref, edge_ref, edge_point_ref, pair_ref, cell
        )
        for k in range(4):
            out_ref[k, place : place + 1, :] = flat[k]


def force_kernel(own, stage, mid_ref, low_ref, high_ref, slope_ref, part_ref, point_ref, edge_ref, edge_point_ref, column_ref, vel_ref, *refs):
    new_vel_ref, pair_ref = refs[0], refs[-1]
    grid = Grid(own)

    def slope(a, b, near):
        index = (a * grid.ey + b) * (own[2] + 2) + near
        return slope_ref[index : index + 1, :]

    for near in range(own[2] + 2):
        for a in range(grid.ex):
            if own[0] == 1 and a == 1:
                continue
            for b in range(grid.ey):
                scale = scale_of(own, mid_ref, low_ref, high_ref, a, b, near)
                pair_ref[:, grid.lanes(a, b, near)] = pair_block(grid, scale, slope(a, b, near))
    for place, cell in enumerate(own_cells(own)):
        point, flat = force_sums(
            grid, own, (-1, 1), mid_ref, slope, part_ref, point_ref, edge_ref, edge_point_ref, pair_ref, cell
        )
        row = slice(place, place + 1)
        flat = [flat[k] + column_ref[k, row, :] for k in range(4)]
        tile = mid_ref[cell[0], cell[1], cell[2]]
        scale = tile[3:4]
        present = jnp.where(scale > 0.5, -2.0, 0.0)
        kick = half_kick * jnp.where(scale > 1.05, 1.6, 1.0)
        for axis in range(3):
            force = present * (flat[axis] - point[axis : axis + 1] * flat[3])
            speed = vel_ref[axis, row, :] + kick * force
            if stage == "middle":
                speed = speed + kick * force
            new_vel_ref[axis, row, :] = speed
            if stage != "last":
                moved = tile[axis : axis + 1] + time_step * speed
                refs[1][place, axis : axis + 1, :] = moved
                if stage == "middle":
                    refs[2][axis, row, :] = moved
        if stage != "last":
            refs[1][place, 3:4, :] = scale


def on_device(positions, velocities, species, counts):
    cx, cy, cz, slots = positions.shape[1:]
    own = (cx, cy, cz)
    cells = cx * cy * cz
    ex, ey = cx + 2, cy + 2
    present = lax.broadcasted_iota(jnp.int32, species.shape, 3) < counts[..., None]
    scale = jnp.where(present, jnp.where(species == 1, ROOT, 1.0), 0.0)
    location = jnp.concatenate([jnp.moveaxis(positions, 0, 3), scale[..., None, :]], axis=3)
    velocity = velocities.reshape(3, cells, slots)
    vmem = pl.BlockSpec(memory_space=pltpu.VMEM)
    flat_shape = jax.ShapeDtypeStruct((3, cells, slots), jnp.float32)

    def block(layers):
        return jax.ShapeDtypeStruct((48, ex * ey * layers * slots), jnp.bfloat16)

    def points(layers):
        return jax.ShapeDtypeStruct((8, ex * ey * layers * slots), jnp.float32)

    def call(kernel, name, operands, out_shape, scratch, pairs):
        return pl.pallas_call(
            kernel,
            out_shape=out_shape,
            in_specs=[vmem] * len(operands),
            out_specs=[vmem] * len(out_shape),
            scratch_shapes=scratch,
            compiler_params=pltpu.CompilerParams(vmem_limit_bytes=GRANT),
            cost_estimate=pl.CostEstimate(
                flops=pairs * slots * slots * 50, bytes_accessed=pairs * slots * slots * 4, transcendentals=0
            ),
            name=name,
        )(*operands)

    def evaluate(location, velocity, stage):
        mid = ring_halo(ring_halo(location, "gy", 1, 1), "gx", 0, 1)
        low, high = neighbours(mid, "gz", 2, 2)
        sums, part, point = call(
            functools.partial(inner_density_kernel, own),
            "inner_density",
            [mid],
            [jax.ShapeDtypeStruct((cells, slots), jnp.float32), block(cz), points(cz)],
            [],
            cells * 18,
        )
        slopes, edge, edge_point = call(
            functools.partial(outer_density_kernel, own),
            "outer_density",
            [mid, low, high, sums, part],
            [jax.ShapeDtypeStruct((cx * cy * (cz + 2), slots), jnp.float32), block(2), points(2)],
            [pltpu.VMEM(block(2).shape, jnp.bfloat16)],
            cells * 36,
        )
        slopes = ring_halo(slopes.reshape(cx, cy, cz + 2, slots), "gy", 1, 1)
        wide = ring_halo(slopes, "gx", 0, 1).reshape(ex * ey * (cz + 2), slots)
        shared = [part, point, edge, edge_point]
        (column,) = call(
            functools.partial(column_force_kernel, own),
            "column_force",
            [mid, low, high, slopes.reshape(cx * ey * (cz + 2), slots), *shared],
            [jax.ShapeDtypeStruct((4, cells, slots), jnp.float32)],
            [pltpu.VMEM(block(cz + 2).shape, jnp.bfloat16)],
            cells * 9,
        )
        out_shape = [flat_shape]
        if stage != "last":
            out_shape.append(jax.ShapeDtypeStruct((cells, 4, slots), jnp.float32))
        if stage == "middle":
            out_shape.append(flat_shape)
        return call(
            functools.partial(force_kernel, own, stage),
            "force_" + stage,
            [mid, low, high, wide, *shared, column, velocity],
            out_shape,
            [pltpu.VMEM(block(cz + 2).shape, jnp.bfloat16)],
            cells * 18,
        )

    velocity, moved = evaluate(location, velocity, "first")
    velocity, moved, new_positions = evaluate(moved.reshape(location.shape), velocity, "middle")
    (velocity,) = evaluate(moved.reshape(location.shape), velocity, "last")
    return new_positions.reshape(positions.shape), velocity.reshape(positions.shape)


def solution(mesh):
    return jax.shard_map(
        on_device,
        mesh=mesh,
        in_specs=(
            P(None, "gx", "gy", "gz", None),
            P(None, "gx", "gy", "gz", None),
            P("gx", "gy", "gz", None),
            P("gx", "gy", "gz"),
        ),
        out_specs=(P(None, "gx", "gy", "gz", None), P(None, "gx", "gy", "gz", None)),
        check_vma=False,
    )
```

```python
import functools

import jax
import jax.numpy as jnp
from jax import lax
from jax.experimental import pallas as pl
from jax.experimental.pallas import tpu as pltpu
from jax.sharding import PartitionSpec as P

time_step = 0.05
half_kick = 0.5 * time_step
LANES = 128
GRANT = 8 * 1024 * 1024
ROOT = 1.3 ** (1.0 / 3.0)
STEPS = (-1, 0, 1)


def neighbours(cells, axis, dim, width):
    count = lax.axis_size(axis)
    size = cells.shape[dim]
    head = lax.slice_in_dim(cells, 0, width, axis=dim)
    tail = lax.slice_in_dim(cells, size - width, size, axis=dim)
    if count == 1:
        return tail, head
    if count == 2 and size == 2 * width:
        other = lax.ppermute(cells, axis, [(0, 1), (1, 0)])
        return (
            lax.slice_in_dim(other, width, size, axis=dim),
            lax.slice_in_dim(other, 0, width, axis=dim),
        )
    below = lax.ppermute(tail, axis, [(i, (i + 1) % count) for i in range(count)])
    above = lax.ppermute(head, axis, [((i + 1) % count, i) for i in range(count)])
    return below, above


def ring_halo(cells, axis, dim, width):
    below, above = neighbours(cells, axis, dim, width)
    return jnp.concatenate([below, cells, above], axis=dim)


def split3(value):
    high = value.astype(jnp.bfloat16).astype(jnp.float32)
    rest = value - high
    middle = rest.astype(jnp.bfloat16).astype(jnp.float32)
    return high, middle, rest - middle


def partner_block(row):
    high, middle, low = split3(row)
    first = jnp.concatenate([high, middle], axis=0).astype(jnp.bfloat16)
    last = jnp.concatenate([low, high], axis=0).astype(jnp.bfloat16)
    return jnp.concatenate([first, first, last], axis=0)


def target_block(row):
    high, middle, low = split3(row)
    stacked = jnp.concatenate([high, high, middle, middle, high, low], axis=0)
    return jnp.transpose(stacked).astype(jnp.bfloat16)


class Grid:
    def __init__(self, own):
        self.cx, self.cy, self.cz = own
        self.ex, self.ey, self.ez = own[0] + 2, own[1] + 2, own[2] + 4
        row = lax.broadcasted_iota(jnp.int32, (8, LANES), 0)
        self.row = row
        self.masks = [(row == k).astype(jnp.float32) for k in range(7)]
        self.spatial = self.masks[0] + self.masks[1] + self.masks[2]

    def own_targets(self):
        return [
            (a, b, c)
            for a in range(1, self.cx + 1)
            for b in range(1, self.cy + 1)
            for c in range(2, self.cz + 2)
        ]

    def edge_targets(self):
        return [
            (a, b, c)
            for a in range(1, self.cx + 1)
            for b in range(1, self.cy + 1)
            for c in (1, self.cz + 2)
        ]

    def slope_row(self, a, b, c):
        return ((a - 1) * self.cy + b - 1) * (self.cz + 2) + c - 1

    def layer(self, c):
        if c in (0, self.ez - 1):
            return "far", int(c > 0)
        if c in (1, self.ez - 2):
            return "edge", int(c > 1)
        return "own", c - 2

    def own_y(self, layer, a, b):
        first, last = max(b - 1, 1), min(b + 1, self.cy)
        return ((layer * self.ex + a) * self.cy + first - 1) * LANES, first, last - first + 1

    def ghost_y(self, side, a, c):
        return ((side * self.ex + a) * self.ez + c) * LANES

    def sides(self, b):
        return [side for side in (0, 1) if b == (1, self.cy)[side]]

    def placed(self, tile, a, b, c):
        m = self.masks
        shift = (
            (a + 0.5 - 0.5 * self.ex) * m[0]
            + (b + 0.5 - 0.5 * self.ey) * m[1]
            + (m[4] + (c + 0.5 - 0.5 * self.ez) * m[2])
        )
        point = jnp.concatenate([tile, jnp.zeros((4, LANES), jnp.float32)], axis=0)
        point = point * self.spatial + shift
        return point, jnp.sum(point * point, axis=0, keepdims=True)

    def partner(self, tile, a, b, c):
        point, bulk = self.placed(tile, a, b, c)
        scale = tile[3:4]
        block = partner_block(jnp.where(self.row == 3, 1.0 - bulk, point) * scale)
        strength = jnp.where(scale > 1.05, 0.4 / ROOT, 0.3)
        return block, jnp.where(self.row == 3, strength, point)

    def target(self, tile, a, b, c):
        point, bulk = self.placed(tile, a, b, c)
        twice = jnp.where(self.row == 4, 2.0 - bulk, 2.0 * point)
        return point, twice + self.masks[3]


def density_of(left_ref, place, sources):
    rows = 64
    sums = []
    for start in range(0, LANES, rows):
        total = jnp.zeros((rows, LANES), jnp.float32)
        for ref, first, count, same in sources:
            near = jnp.dot(
                left_ref[place, start : start + rows, :],
                ref[:, first : first + count * LANES],
                preferred_element_type=jnp.float32,
            )
            for k in range(count):
                part = jnp.maximum(near[:, k * LANES : (k + 1) * LANES], 0.0)
                if k == same:
                    i = lax.broadcasted_iota(jnp.int32, (rows, LANES), 0)
                    j = lax.broadcasted_iota(jnp.int32, (rows, LANES), 1)
                    part = jnp.where(i + start == j, 0.0, part)
                total = total + part * part * part
        sums.append(total)
    return jnp.sum(jnp.transpose(jnp.concatenate(sums, axis=0)), axis=0, keepdims=True)


def own_y_sources(grid, refs, target, layers):
    a, b, c = target
    sources = []
    for r in STEPS:
        which, layer = grid.layer(c + r)
        if which not in layers:
            continue
        for p in STEPS:
            first, start, count = grid.own_y(layer, a + p, b)
            same = b - start if (p == 0 and r == 0) else -1
            sources.append((refs[which], first, count, same))
    return sources


def inner_density_kernel(own, mid_ref, sum_ref, part_ref, point_ref, left_ref):
    grid = Grid(own)
    for c in range(2, grid.cz + 2):
        for a in range(grid.ex):
            for b in range(1, grid.cy + 1):
                first = ((c - 2) * grid.ex + a) * grid.cy * LANES + (b - 1) * LANES
                lanes = slice(first, first + LANES)
                part_ref[:, lanes], point_ref[:, lanes] = grid.partner(mid_ref[a, b - 1, c - 2], a, b, c)
    for place, target in enumerate(grid.own_targets()):
        a, b, c = target
        _, row = grid.target(mid_ref[a, b - 1, c - 2], a, b, c)
        left_ref[place] = target_block(row)
        sources = own_y_sources(grid, {"own": part_ref}, target, ("own",))
        sum_ref[place : place + 1, :] = density_of(left_ref, place, sources)


def outer_density_kernel(own, low_ref, high_ref, inner_ref, part_ref, left_ref, sum_ref, edge_ref, edge_point_ref, edge_left_ref, far_ref):
    grid = Grid(own)

    def tile_of(a, b, c):
        return low_ref[a, b - 1, c] if c < 2 else high_ref[a, b - 1, c - grid.cz - 2]

    for c in (0, 1, grid.ez - 2, grid.ez - 1):
        which, layer = grid.layer(c)
        for a in range(grid.ex):
            for b in range(1, grid.cy + 1):
                first = ((layer * grid.ex + a) * grid.cy + b - 1) * LANES
                lanes = slice(first, first + LANES)
                block, point = grid.partner(tile_of(a, b, c), a, b, c)
                if which == "edge":
                    edge_ref[:, lanes] = block
                    edge_point_ref[:, lanes] = point
                else:
                    far_ref[:, lanes] = block
    refs = {"own": part_ref, "edge": edge_ref, "far": far_ref}
    for place, target in enumerate(grid.edge_targets()):
        _, row = grid.target(tile_of(*target), *target)
        edge_left_ref[place] = target_block(row)
        sources = own_y_sources(grid, refs, target, ("own", "edge", "far"))
        where = grid.slope_row(*target)
        sum_ref[where : where + 1, :] = density_of(edge_left_ref, place, sources)
    for place, target in enumerate(grid.own_targets()):
        where = grid.slope_row(*target)
        density = inner_ref[place : place + 1, :]
        sources = own_y_sources(grid, refs, target, ("edge",))
        if sources:
            density = density + density_of(left_ref, place, sources)
        sum_ref[where : where + 1, :] = density


def last_density_kernel(own, mid_ref, low_ref, high_ref, below_ref, above_ref, sum_ref, left_ref, edge_left_ref, slope_ref, ghost_ref, ghost_point_ref):
    grid = Grid(own)
    for side, ref in enumerate((below_ref, above_ref)):
        for a in range(grid.ex):
            for c in range(grid.ez):
                first = grid.ghost_y(side, a, c)
                lanes = slice(first, first + LANES)
                ghost_ref[:, lanes], ghost_point_ref[:, lanes] = grid.partner(
                    ref[a, 0, c], a, (0, grid.ey - 1)[side], c
                )
    groups = ((grid.own_targets(), left_ref), (grid.edge_targets(), edge_left_ref))
    for targets, rows_ref in groups:
        for place, target in enumerate(targets):
            a, b, c = target
            if c < 2:
                tile = low_ref[a, b - 1, c]
            elif c >= grid.cz + 2:
                tile = high_ref[a, b - 1, c - grid.cz - 2]
            else:
                tile = mid_ref[a, b - 1, c - 2]
            where = grid.slope_row(a, b, c)
            density = sum_ref[where : where + 1, :]
            sources = [
                (ghost_ref, grid.ghost_y(side, a + p, c - 1), 3, -1) for side in grid.sides(b) for p in STEPS
            ]
            if sources:
                density = density + density_of(rows_ref, place, sources)
            present = jnp.where(tile[3:4] > 0.5, -0.5, 0.0)
            slope_ref[where : where + 1, :] = present / jnp.sqrt(density + 1.0)


def pair_block(grid, scale, slope):
    inverse = jnp.where(scale > 1.05, 0.75 / (ROOT * ROOT), 0.75)
    row = jnp.where(grid.row == 5, 0.75 * scale, jnp.where(grid.row == 6, slope * inverse, 0.0))
    return partner_block(row)


def force_of(left_ref, place, sources):
    rows = 32
    sums = [[] for _ in range(4)]
    for start in range(0, LANES, rows):
        total = [jnp.zeros((rows, LANES), jnp.float32) for _ in range(4)]
        for ref, value_ref, first, pair_ref, pair_first, count in sources:
            left = left_ref[place, start : start + rows, :]
            near = jnp.dot(left, ref[:, first : first + count * LANES], preferred_element_type=jnp.float32)
            kappa = jnp.dot(
                left, pair_ref[:, pair_first : pair_first + count * LANES], preferred_element_type=jnp.float32
            )
            for k in range(count):
                part = slice(k * LANES, (k + 1) * LANES)
                lanes = slice(first + k * LANES, first + (k + 1) * LANES)
                s = jnp.maximum(near[:, part], 0.0)
                w = s * (value_ref[3:4, lanes] + s * kappa[:, part])
                total[3] = total[3] + w
                for axis in range(3):
                    total[axis] = total[axis] + w * value_ref[axis : axis + 1, lanes]
        for k in range(4):
            sums[k].append(total[k])
    return [
        jnp.sum(jnp.transpose(jnp.concatenate(parts, axis=0)), axis=0, keepdims=True) for parts in sums
    ]


def own_y_force(grid, columns, scale, slope, left_ref, own_refs, edge_refs, pair_ref, result):
    where = {}
    for c in range(1, grid.ez - 1):
        for a in columns:
            for b in range(1, grid.cy + 1):
                first = where[(a, b, c)] = len(where) * LANES
                pair_ref[:, first : first + LANES] = pair_block(grid, scale(a, b, c), slope(a, b, c))
    refs = {"own": own_refs, "edge": edge_refs}
    for place, (a, b, c) in enumerate(grid.own_targets()):
        sources = []
        for r in STEPS:
            which, layer = grid.layer(c + r)
            for p in STEPS:
                if a + p in columns:
                    first, start, count = grid.own_y(layer, a + p, b)
                    sources.append((*refs[which], first, pair_ref, where[(a + p, start, c + r)], count))
        result(place, force_of(left_ref, place, sources))


def scale_reader(grid, mid_ref, low_ref, high_ref):
    def scale(a, b, c):
        if c < 2:
            return low_ref[a, b - 1, c][3:4]
        if c >= grid.cz + 2:
            return high_ref[a, b - 1, c - grid.cz - 2][3:4]
        return mid_ref[a, b - 1, c - 2][3:4]

    return scale


def column_force_kernel(own, mid_ref, low_ref, high_ref, slope_ref, part_ref, point_ref, edge_ref, edge_point_ref, out_ref, left_ref, pair_ref):
    grid = Grid(own)
    m = grid.masks

    def slope(a, b, c):
        where = grid.slope_row(a, b, c)
        return slope_ref[where : where + 1, :]

    for place, (a, b, c) in enumerate(grid.own_targets()):
        tile = mid_ref[a, b - 1, c - 2]
        _, row = grid.target(tile, a, b, c)
        solute = tile[3:4] > 1.05
        left_ref[place] = target_block(
            row * jnp.where(solute, 0.8, 0.6)
            + slope(a, b, c) * jnp.where(solute, 1.0 / 0.16, 1.0 / 0.09) * m[5]
            + jnp.where(solute, 1.3 / 0.16, 1.0 / 0.09) * m[6]
        )

    def result(place, flat):
        for k in range(4):
            out_ref[k, place : place + 1, :] = flat[k]

    scale = scale_reader(grid, mid_ref, low_ref, high_ref)
    columns = range(1, grid.cx + 1)
    own_y_force(
        grid, columns, scale, slope, left_ref, (part_ref, point_ref), (edge_ref, edge_point_ref), pair_ref, result
    )


def side_force_kernel(own, mid_ref, low_ref, high_ref, slope_ref, part_ref, point_ref, edge_ref, edge_point_ref, column_ref, left_ref, out_ref, pair_ref):
    grid = Grid(own)

    def slope(a, b, c):
        where = grid.slope_row(a + 1, b, c)
        return slope_ref[where : where + 1, :]

    def result(place, flat):
        for k in range(4):
            out_ref[k, place : place + 1, :] = flat[k] + column_ref[k, place : place + 1, :]

    scale = scale_reader(grid, mid_ref, low_ref, high_ref)
    columns = (0, grid.ex - 1)
    own_y_force(
        grid, columns, scale, slope, left_ref, (part_ref, point_ref), (edge_ref, edge_point_ref), pair_ref, result
    )


def last_force_kernel(own, stage, mid_ref, below_ref, above_ref, slope_below_ref, slope_above_ref, ghost_ref, ghost_point_ref, column_ref, left_ref, vel_ref, *refs):
    new_vel_ref, new_loc_ref, pair_ref = refs
    grid = Grid(own)
    near_z = grid.cz + 2
    for side in (0, 1):
        cells_ref, slope_ref = ((below_ref, slope_below_ref), (above_ref, slope_above_ref))[side]
        for a in range(grid.ex):
            for c in range(near_z):
                first = ((side * grid.ex + a) * near_z + c) * LANES
                where = a * near_z + c
                pair_ref[:, first : first + LANES] = pair_block(
                    grid, cells_ref[a, 0, c + 1][3:4], slope_ref[where : where + 1, :]
                )
    for place, (a, b, c) in enumerate(grid.own_targets()):
        sources = [
            (
                ghost_ref,
                ghost_point_ref,
                grid.ghost_y(side, a + p, c - 1),
                pair_ref,
                ((side * grid.ex + a + p) * near_z + c - 2) * LANES,
                3,
            )
            for side in grid.sides(b)
            for p in STEPS
        ]
        row = slice(place, place + 1)
        flat = [column_ref[k, row, :] for k in range(4)]
        if sources:
            flat = [old + new for old, new in zip(flat, force_of(left_ref, place, sources))]
        tile = mid_ref[a, b - 1, c - 2]
        point, _ = grid.placed(tile, a, b, c)
        scale = tile[3:4]
        present = jnp.where(scale > 0.5, -2.0, 0.0)
        kick = half_kick * jnp.where(scale > 1.05, 1.6, 1.0)
        for axis in range(3):
            force = present * (flat[axis] - point[axis : axis + 1] * flat[3])
            speed = vel_ref[axis, row, :] + kick * force
            if stage == "middle":
                speed = speed + kick * force
            new_vel_ref[axis, row, :] = speed
            if stage == "last":
                new_loc_ref[axis, row, :] = tile[axis : axis + 1]
            else:
                new_loc_ref[place, axis : axis + 1, :] = tile[axis : axis + 1] + time_step * speed
        if stage != "last":
            new_loc_ref[place, 3:4, :] = scale


def on_device(positions, velocities, species, counts):
    cx, cy, cz, slots = positions.shape[1:]
    own = (cx, cy, cz)
    cells = cx * cy * cz
    ex, ez = cx + 2, cz + 4
    near = cz + 2
    present = lax.broadcasted_iota(jnp.int32, species.shape, 3) < counts[..., None]
    scale = jnp.where(present, jnp.where(species == 1, ROOT, 1.0), 0.0)
    location = jnp.concatenate([jnp.moveaxis(positions, 0, 3), scale[..., None, :]], axis=3)
    velocity = velocities.reshape(3, cells, slots)
    vmem = pl.BlockSpec(memory_space=pltpu.VMEM)
    flat_shape = jax.ShapeDtypeStruct((3, cells, slots), jnp.float32)

    def block(count):
        return jax.ShapeDtypeStruct((48, count * slots), jnp.bfloat16)

    def points(count):
        return jax.ShapeDtypeStruct((8, count * slots), jnp.float32)

    def rows(count):
        return jax.ShapeDtypeStruct((count, slots), jnp.float32)

    def lefts(count):
        return jax.ShapeDtypeStruct((count, slots, 48), jnp.bfloat16)

    def call(kernel, name, operands, out_shape, pairs, scratch=None):
        return pl.pallas_call(
            kernel,
            out_shape=out_shape,
            in_specs=[vmem] * len(operands),
            out_specs=[vmem] * len(out_shape),
            scratch_shapes=[] if scratch is None else [pltpu.VMEM(scratch.shape, scratch.dtype)],
            compiler_params=pltpu.CompilerParams(vmem_limit_bytes=GRANT),
            cost_estimate=pl.CostEstimate(
                flops=pairs * slots * slots * 50, bytes_accessed=pairs * slots * slots * 4, transcendentals=0
            ),
            name=name,
        )(*operands)

    def evaluate(location, velocity, stage):
        mid = ring_halo(location, "gx", 0, 1)
        low, high = neighbours(mid, "gz", 2, 2)
        tall = jnp.concatenate([low, mid, high], axis=2)
        inner, part, point, left = call(
            functools.partial(inner_density_kernel, own),
            "inner_density",
            [mid],
            [rows(cells), block(ex * cy * cz), points(ex * cy * cz), lefts(cells)],
            cells * 12,
        )
        tall, inner = lax.optimization_barrier((tall, inner))
        below, above = neighbours(tall, "gy", 1, 1)
        sums, edge, edge_point, edge_left = call(
            functools.partial(outer_density_kernel, own),
            "outer_density",
            [low, high, inner, part, left],
            [rows(cx * cy * near), block(ex * cy * 2), points(ex * cy * 2), lefts(cx * cy * 2)],
            cells * 24,
            block(ex * cy * 2),
        )
        slopes, ghost, ghost_point = call(
            functools.partial(last_density_kernel, own),
            "last_density",
            [mid, low, high, below, above, sums, left, edge_left],
            [rows(cx * cy * near), block(2 * ex * ez), points(2 * ex * ez)],
            cells * 18,
        )
        wide = ring_halo(slopes.reshape(cx, cy, near, slots), "gx", 0, 1)
        shared = [part, point, edge, edge_point]
        column, left = call(
            functools.partial(column_force_kernel, own),
            "column_force",
            [mid, low, high, slopes, *shared],
            [jax.ShapeDtypeStruct((4, cells, slots), jnp.float32), lefts(cells)],
            cells * 6,
            block(cx * cy * near),
        )
        wide, column = lax.optimization_barrier((wide, column))
        slope_below, slope_above = neighbours(wide, "gy", 1, 1)
        (column,) = call(
            functools.partial(side_force_kernel, own),
            "side_force",
            [mid, low, high, wide.reshape(ex * cy * near, slots), *shared, column, left],
            [jax.ShapeDtypeStruct((4, cells, slots), jnp.float32)],
            cells * 12,
            block(2 * cy * near),
        )
        moved = flat_shape if stage == "last" else jax.ShapeDtypeStruct((cells, 4, slots), jnp.float32)
        return call(
            functools.partial(last_force_kernel, own, stage),
            "force_" + stage,
            [
                mid,
                below,
                above,
                slope_below.reshape(ex * near, slots),
                slope_above.reshape(ex * near, slots),
                ghost,
                ghost_point,
                column,
                left,
                velocity,
            ],
            [flat_shape, moved],
            cells * 9,
            block(2 * ex * near),
        )

    velocity, moved = evaluate(location, velocity, "first")
    velocity, moved = evaluate(moved.reshape(location.shape), velocity, "middle")
    velocity, new_positions = evaluate(moved.reshape(location.shape), velocity, "last")
    return new_positions.reshape(positions.shape), velocity.reshape(positions.shape)


def solution(mesh):
    return jax.shard_map(
        on_device,
        mesh=mesh,
        in_specs=(
            P(None, "gx", "gy", "gz", None),
            P(None, "gx", "gy", "gz", None),
            P("gx", "gy", "gz", None),
            P("gx", "gy", "gz"),
        ),
        out_specs=(P(None, "gx", "gy", "gz", None), P(None, "gx", "gy", "gz", None)),
        check_vma=False,
    )
```

```python
import functools

import jax
import jax.numpy as jnp
from jax import lax
from jax.experimental import pallas as pl
from jax.experimental.pallas import tpu as pltpu
from jax.sharding import PartitionSpec as P

time_step = 0.05
half_kick = 0.5 * time_step
LANES = 128
GRANT = 8 * 1024 * 1024
ROOT = 1.3 ** (1.0 / 3.0)
STEPS = (-1, 0, 1)
SETS = ("own", "edge", "gown", "gedge")


def neighbours(cells, axis, dim, width):
    count = lax.axis_size(axis)
    size = cells.shape[dim]
    head = lax.slice_in_dim(cells, 0, width, axis=dim)
    tail = lax.slice_in_dim(cells, size - width, size, axis=dim)
    if count == 1:
        return tail, head
    if count == 2 and size == 2 * width:
        other = lax.ppermute(cells, axis, [(0, 1), (1, 0)])
        return (
            lax.slice_in_dim(other, width, size, axis=dim),
            lax.slice_in_dim(other, 0, width, axis=dim),
        )
    below = lax.ppermute(tail, axis, [(i, (i + 1) % count) for i in range(count)])
    above = lax.ppermute(head, axis, [((i + 1) % count, i) for i in range(count)])
    return below, above


def ring_halo(cells, axis, dim, width):
    below, above = neighbours(cells, axis, dim, width)
    return jnp.concatenate([below, cells, above], axis=dim)


def split3(value):
    high = value.astype(jnp.bfloat16).astype(jnp.float32)
    rest = value - high
    middle = rest.astype(jnp.bfloat16).astype(jnp.float32)
    return high, middle, rest - middle


def partner_block(row):
    high, middle, low = split3(row)
    first = jnp.concatenate([high, middle], axis=0).astype(jnp.bfloat16)
    last = jnp.concatenate([low, high], axis=0).astype(jnp.bfloat16)
    return jnp.concatenate([first, first, last], axis=0)


def target_block(row):
    high, middle, low = split3(row)
    stacked = jnp.concatenate([high, high, middle, middle, high, low], axis=0)
    return jnp.transpose(stacked).astype(jnp.bfloat16)


class Grid:
    def __init__(self, own):
        self.cx, self.cy, self.cz = own
        self.ex, self.ey, self.ez = own[0] + 2, own[1] + 2, own[2] + 4
        row = lax.broadcasted_iota(jnp.int32, (8, LANES), 0)
        self.row = row
        self.masks = [(row == k).astype(jnp.float32) for k in range(7)]
        self.spatial = self.masks[0] + self.masks[1] + self.masks[2]
        self.inner = range(1, self.cx + 1)
        self.outer = (0, self.ex - 1)

    def own_targets(self):
        return [(a, b, c) for a in self.inner for b in range(1, self.cy + 1) for c in range(2, self.cz + 2)]

    def edge_targets(self):
        return [(a, b, c) for a in self.inner for b in range(1, self.cy + 1) for c in (1, self.cz + 2)]

    def slope_row(self, a, b, c):
        return ((a - 1) * self.cy + b - 1) * (self.cz + 2) + c - 1

    def place(self, a, b, c):
        if c in (0, self.ez - 1):
            which, layer = "far", int(c > 0)
        elif c in (1, self.ez - 2):
            which, layer = "edge", int(c > 1)
        else:
            which, layer = "own", c - 2
        if 1 <= b <= self.cy:
            return which, (layer * self.ex + a) * self.cy + b - 1
        layers = self.cz if which == "own" else 2
        column = self.outer.index(a) if a in self.outer else a + 1
        return "g" + which, (int(b > 0) * layers + layer) * self.ex + column

    def cells_of(self, which, columns=None):
        columns = range(self.ex) if columns is None else columns
        rows = (0, self.ey - 1) if which[0] == "g" else range(1, self.cy + 1)
        layers = {"n": range(2, self.cz + 2), "e": (1, self.ez - 2), "r": (0, self.ez - 1)}[
            "n" if which.endswith("own") else "e" if which.endswith("edge") else "r"
        ]
        return [(a, b, c) for c in layers for a in columns for b in rows]

    def sources(self, target, sets, columns=None):
        found = {}
        for p in STEPS:
            for q in STEPS:
                for r in STEPS:
                    a, b, c = target[0] + p, target[1] + q, target[2] + r
                    which, index = self.place(a, b, c)
                    if which in sets and (columns is None or a in columns):
                        found.setdefault(which, []).append((index, p == q == r == 0))
        runs = []
        for which in sets:
            entries = sorted(found.get(which, []))
            while entries:
                length = 1
                while length < len(entries) and entries[length][0] == entries[0][0] + length:
                    length += 1
                count = min(length, 2 if length % 2 == 0 else 3)
                same = [k for k in range(count) if entries[k][1]]
                runs.append((which, entries[0][0], count, same[0] if same else -1))
                entries = entries[count:]
        return runs

    def placed(self, tile, a, b, c):
        m = self.masks
        shift = (
            (a + 0.5 - 0.5 * self.ex) * m[0]
            + (b + 0.5 - 0.5 * self.ey) * m[1]
            + (m[4] + (c + 0.5 - 0.5 * self.ez) * m[2])
        )
        point = jnp.concatenate([tile, jnp.zeros((4, LANES), jnp.float32)], axis=0)
        point = point * self.spatial + shift
        return point, jnp.sum(point * point, axis=0, keepdims=True)

    def put_partner(self, tile, cell, refs, point_refs=None):
        which, index = self.place(*cell)
        lanes = slice(index * LANES, (index + 1) * LANES)
        point, bulk = self.placed(tile, *cell)
        scale = tile[3:4]
        refs[which][:, lanes] = partner_block(jnp.where(self.row == 3, 1.0 - bulk, point) * scale)
        if point_refs is not None:
            strength = jnp.where(scale > 1.05, 0.4 / ROOT, 0.3)
            point_refs[which][:, lanes] = jnp.where(
                self.row == 3, strength, jnp.where(self.row == 4, scale, point)
            )

    def target(self, tile, a, b, c):
        point, bulk = self.placed(tile, a, b, c)
        twice = jnp.where(self.row == 4, 2.0 - bulk, 2.0 * point)
        return twice + self.masks[3]


def across(total):
    return jnp.sum(jnp.transpose(total), axis=0, keepdims=True)


def add_density(grid, left_ref, place, runs, refs, before, after):
    rows = 64
    for start in range(0, LANES, rows):
        chunk = slice(start, start + rows)
        total = before(chunk)
        for which, first, count, same in runs:
            near = jnp.dot(
                left_ref[place, chunk, :],
                refs[which][:, first * LANES : (first + count) * LANES],
                preferred_element_type=jnp.float32,
            )
            for k in range(count):
                part = jnp.maximum(near[:, k * LANES : (k + 1) * LANES], 0.0)
                if k == same:
                    i = lax.broadcasted_iota(jnp.int32, (rows, LANES), 0)
                    j = lax.broadcasted_iota(jnp.int32, (rows, LANES), 1)
                    part = jnp.where(i + start == j, 0.0, part)
                cube = part * part * part
                total = cube if total is None else total + cube
        after(chunk, total)


def store_to(ref, place):
    def after(chunk, total):
        ref[place, chunk, :] = total

    return after


def nothing(chunk):
    return None


def prepare_kernel(pos_hbm, vel_hbm, species_hbm, counts_hbm, loc_ref, out_ref, pos_ref, vel_ref, species_ref, counts_ref, arrived):
    copies = [
        pltpu.make_async_copy(source, target, arrived.at[k])
        for k, (source, target) in enumerate(
            ((pos_hbm, pos_ref), (vel_hbm, vel_ref), (species_hbm, species_ref), (counts_hbm, counts_ref))
        )
    ]
    for copy in copies:
        copy.start()
    for copy in copies:
        copy.wait()
    cx, cy, cz = pos_ref.shape[1:4]
    slot = lax.broadcasted_iota(jnp.int32, (1, LANES), 1)
    for a in range(cx):
        for b in range(cy):
            for c in range(cz):
                place = (a * cy + b) * cz + c
                one = slice(c, c + 1)
                for axis in range(3):
                    loc_ref[a, b, c, axis : axis + 1, :] = pos_ref[axis, a, b, one, :]
                    out_ref[axis, place : place + 1, :] = vel_ref[axis, a, b, one, :]
                kind = jnp.where(species_ref[a, b, one, :] == 1, ROOT, 1.0)
                count = jnp.broadcast_to(counts_ref[a, b : b + 1, one], (1, LANES))
                loc_ref[a, b, c, 3:4, :] = jnp.where(slot < count, kind, 0.0)


def inner_density_kernel(own, mid_ref, below_ref, above_ref, sum_ref, part_ref, point_ref, ghost_ref, ghost_point_ref, left_ref):
    grid = Grid(own)
    refs = {"own": part_ref, "gown": ghost_ref}
    point_refs = {"own": point_ref, "gown": ghost_point_ref}
    for a, b, c in grid.cells_of("own"):
        grid.put_partner(mid_ref[a, b - 1, c - 2], (a, b, c), refs, point_refs)
    for a, b, c in grid.cells_of("gown"):
        tile = (below_ref if b == 0 else above_ref)[a, 0, c - 2]
        grid.put_partner(tile, (a, b, c), refs, point_refs)
    for place, (a, b, c) in enumerate(grid.own_targets()):
        left_ref[place] = target_block(grid.target(mid_ref[a, b - 1, c - 2], a, b, c))
        runs = grid.sources((a, b, c), ("own", "gown"))
        add_density(grid, left_ref, place, runs, refs, nothing, store_to(sum_ref, place))


def outer_density_kernel(own, low_ref, high_ref, inner_ref, part_ref, ghost_ref, left_ref, own_sum_ref, edge_sum_ref, edge_ref, edge_point_ref, edge_left_ref, far_ref):
    grid = Grid(own)
    refs = {"own": part_ref, "gown": ghost_ref, "edge": edge_ref, "far": far_ref}

    def tile_of(a, b, c):
        return low_ref[a, b - 1, c] if c < 2 else high_ref[a, b - 1, c - grid.cz - 2]

    for cell in grid.cells_of("edge"):
        grid.put_partner(tile_of(*cell), cell, refs, {"edge": edge_point_ref})
    for cell in grid.cells_of("far"):
        grid.put_partner(tile_of(*cell), cell, refs)
    for place, cell in enumerate(grid.edge_targets()):
        edge_left_ref[place] = target_block(grid.target(tile_of(*cell), *cell))
        runs = grid.sources(cell, ("own", "gown", "edge", "far"))
        add_density(grid, edge_left_ref, place, runs, refs, nothing, store_to(edge_sum_ref, place))
    for place, cell in enumerate(grid.own_targets()):
        runs = grid.sources(cell, ("edge",))
        before = lambda chunk, place=place: inner_ref[place, chunk, :]
        add_density(grid, left_ref, place, runs, refs, before, store_to(own_sum_ref, place))


def last_density_kernel(own, mid_ref, low_ref, high_ref, below_ref, above_ref, own_sum_ref, edge_sum_ref, left_ref, edge_left_ref, slope_ref, weight_ref, ghost_ref, ghost_point_ref, far_ref):
    grid = Grid(own)
    refs = {"gedge": ghost_ref, "gfar": far_ref}
    for which in ("gedge", "gfar"):
        for a, b, c in grid.cells_of(which):
            tile = (below_ref if b == 0 else above_ref)[a, 0, c if c < 2 else c - grid.cz]
            grid.put_partner(tile, (a, b, c), refs, {"gedge": ghost_point_ref} if which == "gedge" else None)
    groups = ((grid.own_targets(), own_sum_ref, left_ref), (grid.edge_targets(), edge_sum_ref, edge_left_ref))
    for targets, sum_ref, rows_ref in groups:
        for place, (a, b, c) in enumerate(targets):
            if c < 2:
                tile = low_ref[a, b - 1, c]
            elif c >= grid.cz + 2:
                tile = high_ref[a, b - 1, c - grid.cz - 2]
            else:
                tile = mid_ref[a, b - 1, c - 2]
            runs = grid.sources((a, b, c), ("gedge", "gfar"))
            parts = []
            before = lambda chunk, place=place, sum_ref=sum_ref: sum_ref[place, chunk, :]
            add_density(grid, rows_ref, place, runs, refs, before, lambda chunk, total: parts.append(total))
            density = across(jnp.concatenate(parts, axis=0))
            scale = tile[3:4]
            slope = jnp.where(scale > 0.5, -0.5, 0.0) / jnp.sqrt(density + 1.0)
            where = grid.slope_row(a, b, c)
            slope_ref[where : where + 1, :] = slope
            weight_ref[where : where + 1, :] = slope * jnp.where(scale > 1.05, 0.75 / (ROOT * ROOT), 0.75)


def put_pair(grid, cell, point_refs, pair_refs, weight):
    which, index = grid.place(*cell)
    lanes = slice(index * LANES, (index + 1) * LANES)
    scale = point_refs[which][4:5, lanes]
    row = jnp.where(grid.row == 5, 0.75 * scale, jnp.where(grid.row == 6, weight, 0.0))
    high = row.astype(jnp.bfloat16).astype(jnp.float32)
    first = jnp.concatenate([high, row - high], axis=0).astype(jnp.bfloat16)
    last = jnp.concatenate([jnp.zeros((8, LANES), jnp.float32), high], axis=0).astype(jnp.bfloat16)
    pair_refs[which][:, lanes] = jnp.concatenate([first, first, last], axis=0)


def add_force(left_ref, place, runs, refs, point_refs, pair_refs, before, after):
    rows = 32
    for start in range(0, LANES, rows):
        chunk = slice(start, start + rows)
        total = before(chunk)
        left = left_ref[place, chunk, :]
        for which, first, count, _ in runs:
            span = slice(first * LANES, (first + count) * LANES)
            near = jnp.dot(left, refs[which][:, span], preferred_element_type=jnp.float32)
            kappa = jnp.dot(left, pair_refs[which][:, span], preferred_element_type=jnp.float32)
            value_ref = point_refs[which]
            for k in range(count):
                part = slice(k * LANES, (k + 1) * LANES)
                lanes = slice((first + k) * LANES, (first + k + 1) * LANES)
                s = jnp.maximum(near[:, part], 0.0)
                w = s * (value_ref[3:4, lanes] + s * kappa[:, part])
                new = [w * value_ref[axis : axis + 1, lanes] for axis in range(3)] + [w]
                total = new if total is None else [old + more for old, more in zip(total, new)]
        after(chunk, total)


def store_four(ref, place):
    def after(chunk, total):
        for k in range(4):
            ref[k, place, chunk, :] = total[k]

    return after


def load_four(ref, place):
    def before(chunk):
        return [ref[k, place, chunk, :] for k in range(4)]

    return before


def row_of(ref, index):
    return ref[index : index + 1, :]


def column_force_kernel(own, *all_refs):
    mid_ref, slope_ref, weight_ref, below_ref, above_ref = all_refs[:5]
    refs = dict(zip(SETS, all_refs[5:9]))
    point_refs = dict(zip(SETS, all_refs[9:13]))
    out_ref, left_ref = all_refs[13:15]
    pair_refs = dict(zip(SETS, all_refs[15:]))
    grid = Grid(own)
    m = grid.masks
    near = grid.cz + 2
    for which in SETS:
        for a, b, c in grid.cells_of(which, grid.inner):
            if which[0] == "g":
                weight = row_of(below_ref if b == 0 else above_ref, (a - 1) * near + c - 1)
            else:
                weight = row_of(weight_ref, grid.slope_row(a, b, c))
            put_pair(grid, (a, b, c), point_refs, pair_refs, weight)
    for place, (a, b, c) in enumerate(grid.own_targets()):
        tile = mid_ref[a, b - 1, c - 2]
        solute = tile[3:4] > 1.05
        left_ref[place] = target_block(
            grid.target(tile, a, b, c) * jnp.where(solute, 0.8, 0.6)
            + row_of(slope_ref, grid.slope_row(a, b, c)) * jnp.where(solute, 1.0 / 0.16, 1.0 / 0.09) * m[5]
            + jnp.where(solute, 1.3 / 0.16, 1.0 / 0.09) * m[6]
        )
        runs = grid.sources((a, b, c), SETS, grid.inner)
        add_force(left_ref, place, runs, refs, point_refs, pair_refs, nothing, store_four(out_ref, place))


def side_force_kernel(own, below_ref, above_ref, part_ref, edge_ref, point_ref, edge_point_ref, column_ref, left_ref, out_ref, pair_ref, edge_pair_ref):
    grid = Grid(own)
    refs = {"own": part_ref, "edge": edge_ref}
    point_refs = {"own": point_ref, "edge": edge_point_ref}
    pair_refs = {"own": pair_ref, "edge": edge_pair_ref}
    for which in refs:
        for a, b, c in grid.cells_of(which, grid.outer):
            weight = row_of(below_ref if a == 0 else above_ref, grid.slope_row(1, b, c))
            put_pair(grid, (a, b, c), point_refs, pair_refs, weight)
    for place, cell in enumerate(grid.own_targets()):
        runs = grid.sources(cell, tuple(refs), grid.outer)
        before, after = load_four(column_ref, place), store_four(out_ref, place)
        add_force(left_ref, place, runs, refs, point_refs, pair_refs, before, after)


def last_force_kernel(own, stage, mid_ref, below_ref, above_ref, ghost_ref, ghost_edge_ref, ghost_point_ref, ghost_edge_point_ref, column_ref, left_ref, vel_ref, *out_refs):
    new_vel_ref, new_loc_ref, pair_ref, edge_pair_ref = out_refs
    grid = Grid(own)
    near = grid.cz + 2
    refs = {"gown": ghost_ref, "gedge": ghost_edge_ref}
    point_refs = {"gown": ghost_point_ref, "gedge": ghost_edge_point_ref}
    pair_refs = {"gown": pair_ref, "gedge": edge_pair_ref}
    for which in refs:
        for a, b, c in grid.cells_of(which, grid.outer):
            weight = row_of(below_ref if b == 0 else above_ref, int(a > 0) * near + c - 1)
            put_pair(grid, (a, b, c), point_refs, pair_refs, weight)
    for place, (a, b, c) in enumerate(grid.own_targets()):
        parts = []
        runs = grid.sources((a, b, c), tuple(refs), grid.outer)
        after = lambda chunk, total: parts.append(total)
        add_force(left_ref, place, runs, refs, point_refs, pair_refs, load_four(column_ref, place), after)
        flat = [across(jnp.concatenate([part[k] for part in parts], axis=0)) for k in range(4)]
        row = slice(place, place + 1)
        tile = mid_ref[a, b - 1, c - 2]
        point, _ = grid.placed(tile, a, b, c)
        scale = tile[3:4]
        present = jnp.where(scale > 0.5, -2.0, 0.0)
        kick = half_kick * jnp.where(scale > 1.05, 1.6, 1.0)
        for axis in range(3):
            force = present * (flat[axis] - point[axis : axis + 1] * flat[3])
            speed = vel_ref[axis, row, :] + kick * force
            if stage == "middle":
                speed = speed + kick * force
            new_vel_ref[axis, row, :] = speed
            if stage == "last":
                new_loc_ref[axis, row, :] = tile[axis : axis + 1]
            else:
                new_loc_ref[place, axis : axis + 1, :] = tile[axis : axis + 1] + time_step * speed
        if stage != "last":
            new_loc_ref[place, 3:4, :] = scale


def on_device(positions, velocities, species, counts):
    cx, cy, cz, slots = positions.shape[1:]
    own = (cx, cy, cz)
    cells = cx * cy * cz
    ex, near = cx + 2, cz + 2
    vmem = pl.BlockSpec(memory_space=pltpu.VMEM)
    flat_shape = jax.ShapeDtypeStruct((3, cells, slots), jnp.float32)
    sizes = {"own": ex * cy * cz, "edge": ex * cy * 2, "gown": 2 * ex * cz, "gedge": 2 * ex * 2}

    def block(which):
        return jax.ShapeDtypeStruct((48, sizes[which] * slots), jnp.bfloat16)

    def points(which):
        return jax.ShapeDtypeStruct((8, sizes[which] * slots), jnp.float32)

    def sums(*count):
        return jax.ShapeDtypeStruct((*count, slots, slots), jnp.float32)

    def rows(count):
        return jax.ShapeDtypeStruct((count, slots), jnp.float32)

    def lefts(count):
        return jax.ShapeDtypeStruct((count, slots, 48), jnp.bfloat16)

    def call(kernel, name, operands, out_shape, pairs, scratch=()):
        return pl.pallas_call(
            kernel,
            out_shape=out_shape,
            in_specs=[vmem] * len(operands),
            out_specs=[vmem] * len(out_shape),
            scratch_shapes=[pltpu.VMEM(item.shape, item.dtype) for item in scratch],
            compiler_params=pltpu.CompilerParams(vmem_limit_bytes=GRANT),
            cost_estimate=pl.CostEstimate(
                flops=pairs * slots * slots * 50, bytes_accessed=pairs * slots * slots * 4, transcendentals=0
            ),
            name=name,
        )(*operands)

    def evaluate(location, velocity, stage):
        mid = ring_halo(location, "gx", 0, 1)
        mid_below, mid_above = neighbours(mid, "gy", 1, 1)
        low, high = neighbours(mid, "gz", 2, 2)
        inner, part, point, ghost, ghost_point, left = call(
            functools.partial(inner_density_kernel, own),
            "inner_density",
            [mid, mid_below, mid_above],
            [sums(cells), block("own"), points("own"), block("gown"), points("gown"), lefts(cells)],
            cells * 18,
        )
        tall, inner = lax.optimization_barrier((jnp.concatenate([low, high], axis=2), inner))
        below, above = neighbours(tall, "gy", 1, 1)
        own_sum, edge_sum, edge, edge_point, edge_left = call(
            functools.partial(outer_density_kernel, own),
            "outer_density",
            [low, high, inner, part, ghost, left],
            [sums(cells), sums(cx * cy * 2), block("edge"), points("edge"), lefts(cx * cy * 2)],
            cells * 27,
            [block("edge")],
        )
        slopes, weights, ghost_edge, ghost_edge_point = call(
            functools.partial(last_density_kernel, own),
            "last_density",
            [mid, low, high, below, above, own_sum, edge_sum, left, edge_left],
            [rows(cx * cy * near), rows(cx * cy * near), block("gedge"), points("gedge")],
            cells * 9,
            [block("gedge")],
        )
        weights = weights.reshape(cx, cy, near, slots)
        weight_below, weight_above = neighbours(weights, "gy", 1, 1)
        side_below, side_above = neighbours(weights, "gx", 0, 1)
        column, left = call(
            functools.partial(column_force_kernel, own),
            "column_force",
            [
                mid,
                slopes,
                weights.reshape(cx * cy * near, slots),
                weight_below.reshape(cx * near, slots),
                weight_above.reshape(cx * near, slots),
                *(part, edge, ghost, ghost_edge),
                *(point, edge_point, ghost_point, ghost_edge_point),
            ],
            [sums(4, cells), lefts(cells)],
            cells * 9,
            [block(which) for which in SETS],
        )
        sides, column = lax.optimization_barrier((jnp.concatenate([side_below, side_above], axis=0), column))
        corner_below, corner_above = neighbours(sides, "gy", 1, 1)
        (column,) = call(
            functools.partial(side_force_kernel, own),
            "side_force",
            [
                side_below.reshape(cy * near, slots),
                side_above.reshape(cy * near, slots),
                *(part, edge, point, edge_point, column, left),
            ],
            [sums(4, cells)],
            cells * 12,
            [block("own"), block("edge")],
        )
        moved = flat_shape if stage == "last" else jax.ShapeDtypeStruct((cells, 4, slots), jnp.float32)
        return call(
            functools.partial(last_force_kernel, own, stage),
            "force_" + stage,
            [
                mid,
                corner_below.reshape(2 * near, slots),
                corner_above.reshape(2 * near, slots),
                *(ghost, ghost_edge, ghost_point, ghost_edge_point, column, left, velocity),
            ],
            [flat_shape, moved],
            cells * 6,
            [block("gown"), block("gedge")],
        )

    arrays = [pltpu.with_memory_space_constraint(x, pltpu.HBM) for x in (positions, velocities, species, counts)]
    location, velocity = pl.pallas_call(
        prepare_kernel,
        out_shape=[jax.ShapeDtypeStruct((cx, cy, cz, 4, slots), jnp.float32), flat_shape],
        in_specs=[pl.BlockSpec(memory_space=pltpu.HBM)] * 4,
        out_specs=[vmem] * 2,
        scratch_shapes=[pltpu.VMEM(array.shape, array.dtype) for array in arrays] + [pltpu.SemaphoreType.DMA((4,))],
        compiler_params=pltpu.CompilerParams(vmem_limit_bytes=GRANT),
        name="prepare",
    )(*arrays)
    velocity, moved = evaluate(location, velocity, "first")
    velocity, moved = evaluate(moved.reshape(location.shape), velocity, "middle")
    velocity, new_positions = evaluate(moved.reshape(location.shape), velocity, "last")
    return new_positions.reshape(positions.shape), velocity.reshape(positions.shape)


def solution(mesh):
    return jax.shard_map(
        on_device,
        mesh=mesh,
        in_specs=(
            P(None, "gx", "gy", "gz", None),
            P(None, "gx", "gy", "gz", None),
            P("gx", "gy", "gz", None),
            P("gx", "gy", "gz"),
        ),
        out_specs=(P(None, "gx", "gy", "gz", None), P(None, "gx", "gy", "gz", None)),
        check_vma=False,
    )
```

```python
import functools

import jax
import jax.numpy as jnp
from jax import lax
from jax.experimental import pallas as pl
from jax.experimental.pallas import tpu as pltpu
from jax.sharding import PartitionSpec as P


time_step = 0.05
half_kick = 0.5 * time_step
LANES = 128
GRANT = 8 * 1024 * 1024
ROOT = 1.3 ** (1.0 / 3.0)
STEPS = (-1, 0, 1)
SETS = ("own", "edge", "gown", "gedge")


def neighbours(cells, axis, dim, width):
    count = lax.axis_size(axis)
    size = cells.shape[dim]
    head = lax.slice_in_dim(cells, 0, width, axis=dim)
    tail = lax.slice_in_dim(cells, size - width, size, axis=dim)
    if count == 1:
        return tail, head
    if count == 2 and size == 2 * width:
        other = lax.ppermute(cells, axis, [(0, 1), (1, 0)])
        return (
            lax.slice_in_dim(other, width, size, axis=dim),
            lax.slice_in_dim(other, 0, width, axis=dim),
        )
    below = lax.ppermute(tail, axis, [(i, (i + 1) % count) for i in range(count)])
    above = lax.ppermute(head, axis, [((i + 1) % count, i) for i in range(count)])
    return below, above


def ring_halo(cells, axis, dim, width):
    below, above = neighbours(cells, axis, dim, width)
    return jnp.concatenate([below, cells, above], axis=dim)


def split3(value):
    high = value.astype(jnp.bfloat16).astype(jnp.float32)
    rest = value - high
    middle = rest.astype(jnp.bfloat16).astype(jnp.float32)
    return high, middle, rest - middle


def partner_block(row):
    high, middle, low = split3(row)
    first = jnp.concatenate([high, middle], axis=0).astype(jnp.bfloat16)
    last = jnp.concatenate([low, high], axis=0).astype(jnp.bfloat16)
    return jnp.concatenate([first, first, last], axis=0)


def target_block(row):
    high, middle, low = split3(row)
    stacked = jnp.concatenate([high, high, middle, middle, high, low], axis=0)
    return jnp.transpose(stacked).astype(jnp.bfloat16)


class Grid:
    def __init__(self, own):
        self.cx, self.cy, self.cz = own
        self.ex, self.ey, self.ez = own[0] + 2, own[1] + 2, own[2] + 4
        row = lax.broadcasted_iota(jnp.int32, (8, LANES), 0)
        self.row = row
        self.masks = [(row == k).astype(jnp.float32) for k in range(7)]
        self.spatial = self.masks[0] + self.masks[1] + self.masks[2]
        self.inner = range(1, self.cx + 1)
        self.outer = (0, self.ex - 1)

    def own_targets(self):
        return [(a, b, c) for a in self.inner for b in range(1, self.cy + 1) for c in range(2, self.cz + 2)]

    def edge_targets(self):
        return [(a, b, c) for a in self.inner for b in range(1, self.cy + 1) for c in (1, self.cz + 2)]

    def slope_row(self, a, b, c):
        return ((a - 1) * self.cy + b - 1) * (self.cz + 2) + c - 1

    def place(self, a, b, c):
        if c in (0, self.ez - 1):
            which, layer = "far", int(c > 0)
        elif c in (1, self.ez - 2):
            which, layer = "edge", int(c > 1)
        else:
            which, layer = "own", c - 2
        if 1 <= b <= self.cy:
            return which, (layer * self.ex + a) * self.cy + b - 1
        layers = self.cz if which == "own" else 2
        column = self.outer.index(a) if a in self.outer else a + 1
        return "g" + which, (int(b > 0) * layers + layer) * self.ex + column

    def cells_of(self, which, columns=None):
        columns = range(self.ex) if columns is None else columns
        rows = (0, self.ey - 1) if which[0] == "g" else range(1, self.cy + 1)
        layers = {"n": range(2, self.cz + 2), "e": (1, self.ez - 2), "r": (0, self.ez - 1)}[
            "n" if which.endswith("own") else "e" if which.endswith("edge") else "r"
        ]
        return [(a, b, c) for c in layers for a in columns for b in rows]

    def sources(self, target, sets, columns=None):
        found = {}
        for p in STEPS:
            for q in STEPS:
                for r in STEPS:
                    a, b, c = target[0] + p, target[1] + q, target[2] + r
                    which, index = self.place(a, b, c)
                    if which in sets and (columns is None or a in columns):
                        found.setdefault(which, []).append((index, p == q == r == 0))
        runs = []
        for which in sets:
            entries = sorted(found.get(which, []))
            while entries:
                length = 1
                while length < len(entries) and entries[length][0] == entries[0][0] + length:
                    length += 1
                count = min(length, 2 if length % 2 == 0 else 3)
                same = [k for k in range(count) if entries[k][1]]
                runs.append((which, entries[0][0], count, same[0] if same else -1))
                entries = entries[count:]
        return runs

    def placed(self, tile, a, b, c):
        m = self.masks
        shift = (
            (a + 0.5 - 0.5 * self.ex) * m[0]
            + (b + 0.5 - 0.5 * self.ey) * m[1]
            + (m[4] + (c + 0.5 - 0.5 * self.ez) * m[2])
        )
        point = jnp.concatenate([tile, jnp.zeros((4, LANES), jnp.float32)], axis=0)
        point = point * self.spatial + shift
        return point, jnp.sum(point * point, axis=0, keepdims=True)

    def put_partner(self, tile, cell, refs, point_refs=None):
        which, index = self.place(*cell)
        lanes = slice(index * LANES, (index + 1) * LANES)
        point, bulk = self.placed(tile, *cell)
        scale = tile[3:4]
        refs[which][:, lanes] = partner_block(jnp.where(self.row == 3, 1.0 - bulk, point) * scale)
        if point_refs is not None:
            strength = jnp.where(scale > 1.05, 0.4 / ROOT, 0.3)
            point_refs[which][:, lanes] = jnp.where(
                self.row == 3, strength, jnp.where(self.row == 4, scale, point)
            )

    def target(self, tile, a, b, c):
        point, bulk = self.placed(tile, a, b, c)
        twice = jnp.where(self.row == 4, 2.0 - bulk, 2.0 * point)
        return twice + self.masks[3]


def across(total):
    return jnp.sum(jnp.transpose(total), axis=0, keepdims=True)


def add_density(left_ref, place, runs, refs, before, after):
    rows = 128
    for start in range(0, LANES, rows):
        chunk = slice(start, start + rows)
        total = before(chunk)
        for which, first, count, same in runs:
            near = jnp.dot(
                left_ref[place, chunk, :],
                refs[which][:, first * LANES : (first + count) * LANES],
                preferred_element_type=jnp.float32,
            )
            for k in range(count):
                part = jnp.maximum(near[:, k * LANES : (k + 1) * LANES], 0.0)
                if k == same:
                    i = lax.broadcasted_iota(jnp.int32, (rows, LANES), 0)
                    j = lax.broadcasted_iota(jnp.int32, (rows, LANES), 1)
                    part = jnp.where(i + start == j, 0.0, part)
                cube = part * part * part
                total = cube if total is None else total + cube
        after(chunk, total)


def store_to(ref, place):
    def after(chunk, total):
        ref[place, chunk, :] = total

    return after


def nothing(chunk):
    return None


def prepare_kernel(pos_hbm, vel_hbm, species_hbm, counts_hbm, loc_ref, out_ref, pos_ref, vel_ref, species_ref, counts_ref, arrived):
    copies = [
        pltpu.make_async_copy(source, target, arrived.at[k])
        for k, (source, target) in enumerate(
            ((pos_hbm, pos_ref), (vel_hbm, vel_ref), (species_hbm, species_ref), (counts_hbm, counts_ref))
        )
    ]
    for copy in copies:
        copy.start()
    for copy in copies:
        copy.wait()
    cx, cy, cz = pos_ref.shape[1:4]
    slot = lax.broadcasted_iota(jnp.int32, (1, LANES), 1)
    for a in range(cx):
        for b in range(cy):
            for c in range(cz):
                place = (a * cy + b) * cz + c
                one = slice(c, c + 1)
                for axis in range(3):
                    loc_ref[a, b, c, axis : axis + 1, :] = pos_ref[axis, a, b, one, :]
                    out_ref[axis, place : place + 1, :] = vel_ref[axis, a, b, one, :]
                kind = jnp.where(species_ref[a, b, one, :] == 1, ROOT, 1.0)
                count = jnp.broadcast_to(counts_ref[a, b : b + 1, one], (1, LANES))
                loc_ref[a, b, c, 3:4, :] = jnp.where(slot < count, kind, 0.0)


def inner_density_kernel(own, mid_ref, below_ref, above_ref, sum_ref, part_ref, point_ref, ghost_ref, ghost_point_ref, left_ref):
    grid = Grid(own)
    refs = {"own": part_ref, "gown": ghost_ref}
    point_refs = {"own": point_ref, "gown": ghost_point_ref}
    for a, b, c in grid.cells_of("own"):
        grid.put_partner(mid_ref[a, b - 1, c - 2], (a, b, c), refs, point_refs)
    for a, b, c in grid.cells_of("gown"):
        tile = (below_ref if b == 0 else above_ref)[a, 0, c - 2]
        grid.put_partner(tile, (a, b, c), refs, point_refs)
    for place, (a, b, c) in enumerate(grid.own_targets()):
        left_ref[place] = target_block(grid.target(mid_ref[a, b - 1, c - 2], a, b, c))
        runs = grid.sources((a, b, c), ("own", "gown"))
        add_density(left_ref, place, runs, refs, nothing, store_to(sum_ref, place))


def outer_density_kernel(own, low_ref, high_ref, inner_ref, part_ref, ghost_ref, left_ref, own_sum_ref, edge_sum_ref, edge_ref, edge_point_ref, edge_left_ref, far_ref):
    grid = Grid(own)
    refs = {"own": part_ref, "gown": ghost_ref, "edge": edge_ref, "far": far_ref}

    def tile_of(a, b, c):
        return low_ref[a, b - 1, c] if c < 2 else high_ref[a, b - 1, c - grid.cz - 2]

    for cell in grid.cells_of("edge"):
        grid.put_partner(tile_of(*cell), cell, refs, {"edge": edge_point_ref})
    for cell in grid.cells_of("far"):
        grid.put_partner(tile_of(*cell), cell, refs)
    for place, cell in enumerate(grid.edge_targets()):
        edge_left_ref[place] = target_block(grid.target(tile_of(*cell), *cell))
        runs = grid.sources(cell, ("own", "gown", "edge", "far"))
        add_density(edge_left_ref, place, runs, refs, nothing, store_to(edge_sum_ref, place))
    for place, cell in enumerate(grid.own_targets()):
        runs = grid.sources(cell, ("edge",))
        before = lambda chunk, place=place: inner_ref[place, chunk, :]
        add_density(left_ref, place, runs, refs, before, store_to(own_sum_ref, place))


def last_density_kernel(own, mid_ref, low_ref, high_ref, below_ref, above_ref, own_sum_ref, edge_sum_ref, left_ref, edge_left_ref, slope_ref, weight_ref, ghost_ref, ghost_point_ref, far_ref):
    grid = Grid(own)
    refs = {"gedge": ghost_ref, "gfar": far_ref}
    for which in ("gedge", "gfar"):
        for a, b, c in grid.cells_of(which):
            tile = (below_ref if b == 0 else above_ref)[a, 0, c if c < 2 else c - grid.cz]
            grid.put_partner(tile, (a, b, c), refs, {"gedge": ghost_point_ref} if which == "gedge" else None)
    groups = ((grid.own_targets(), own_sum_ref, left_ref), (grid.edge_targets(), edge_sum_ref, edge_left_ref))
    for targets, sum_ref, rows_ref in groups:
        for place, (a, b, c) in enumerate(targets):
            if c < 2:
                tile = low_ref[a, b - 1, c]
            elif c >= grid.cz + 2:
                tile = high_ref[a, b - 1, c - grid.cz - 2]
            else:
                tile = mid_ref[a, b - 1, c - 2]
            runs = grid.sources((a, b, c), ("gedge", "gfar"))
            parts = []
            before = lambda chunk, place=place, sum_ref=sum_ref: sum_ref[place, chunk, :]
            add_density(rows_ref, place, runs, refs, before, lambda chunk, total: parts.append(total))
            density = across(jnp.concatenate(parts, axis=0))
            scale = tile[3:4]
            slope = jnp.where(scale > 0.5, -0.5, 0.0) / jnp.sqrt(density + 1.0)
            where = grid.slope_row(a, b, c)
            slope_ref[where : where + 1, :] = slope
            weight_ref[where : where + 1, :] = slope * jnp.where(scale > 1.05, 0.75 / (ROOT * ROOT), 0.75)


def put_pair(grid, cell, point_refs, pair_refs, weight):
    which, index = grid.place(*cell)
    lanes = slice(index * LANES, (index + 1) * LANES)
    scale = point_refs[which][4:5, lanes]
    row = jnp.where(grid.row == 5, 0.75 * scale, jnp.where(grid.row == 6, weight, 0.0))
    high = row.astype(jnp.bfloat16).astype(jnp.float32)
    first = jnp.concatenate([high, row - high], axis=0).astype(jnp.bfloat16)
    last = jnp.concatenate([jnp.zeros((8, LANES), jnp.float32), high], axis=0).astype(jnp.bfloat16)
    pair_refs[which][:, lanes] = jnp.concatenate([first, first, last], axis=0)


def add_force(left_ref, place, runs, refs, point_refs, pair_refs, before, after):
    rows = 128
    for start in range(0, LANES, rows):
        chunk = slice(start, start + rows)
        total = before(chunk)
        left = left_ref[place, chunk, :]
        for which, first, count, _ in runs:
            span = slice(first * LANES, (first + count) * LANES)
            near = jnp.dot(left, refs[which][:, span], preferred_element_type=jnp.float32)
            kappa = jnp.dot(left, pair_refs[which][:, span], preferred_element_type=jnp.float32)
            value_ref = point_refs[which]
            for k in range(count):
                part = slice(k * LANES, (k + 1) * LANES)
                lanes = slice((first + k) * LANES, (first + k + 1) * LANES)
                s = jnp.maximum(near[:, part], 0.0)
                w = s * (value_ref[3:4, lanes] + s * kappa[:, part])
                new = [w * value_ref[axis : axis + 1, lanes] for axis in range(3)] + [w]
                total = new if total is None else [old + more for old, more in zip(total, new)]
        after(chunk, total)


def store_four(ref, place):
    def after(chunk, total):
        for k in range(4):
            ref[k, place, chunk, :] = total[k]

    return after


def load_four(ref, place):
    def before(chunk):
        return [ref[k, place, chunk, :] for k in range(4)]

    return before


def row_of(ref, index):
    return ref[index : index + 1, :]


def column_force_kernel(own, *all_refs):
    mid_ref, slope_ref, weight_ref, below_ref, above_ref = all_refs[:5]
    refs = dict(zip(SETS, all_refs[5:9]))
    point_refs = dict(zip(SETS, all_refs[9:13]))
    out_ref, left_ref = all_refs[13:15]
    pair_refs = dict(zip(SETS, all_refs[15:]))
    grid = Grid(own)
    m = grid.masks
    near = grid.cz + 2
    for which in SETS:
        for a, b, c in grid.cells_of(which, grid.inner):
            if which[0] == "g":
                weight = row_of(below_ref if b == 0 else above_ref, (a - 1) * near + c - 1)
            else:
                weight = row_of(weight_ref, grid.slope_row(a, b, c))
            put_pair(grid, (a, b, c), point_refs, pair_refs, weight)
    for place, (a, b, c) in enumerate(grid.own_targets()):
        tile = mid_ref[a, b - 1, c - 2]
        solute = tile[3:4] > 1.05
        left_ref[place] = target_block(
            grid.target(tile, a, b, c) * jnp.where(solute, 0.8, 0.6)
            + row_of(slope_ref, grid.slope_row(a, b, c)) * jnp.where(solute, 1.0 / 0.16, 1.0 / 0.09) * m[5]
            + jnp.where(solute, 1.3 / 0.16, 1.0 / 0.09) * m[6]
        )
        runs = grid.sources((a, b, c), SETS, grid.inner)
        add_force(left_ref, place, runs, refs, point_refs, pair_refs, nothing, store_four(out_ref, place))


def side_force_kernel(own, below_ref, above_ref, part_ref, edge_ref, point_ref, edge_point_ref, column_ref, left_ref, out_ref, pair_ref, edge_pair_ref):
    grid = Grid(own)
    refs = {"own": part_ref, "edge": edge_ref}
    point_refs = {"own": point_ref, "edge": edge_point_ref}
    pair_refs = {"own": pair_ref, "edge": edge_pair_ref}
    for which in refs:
        for a, b, c in grid.cells_of(which, grid.outer):
            weight = row_of(below_ref if a == 0 else above_ref, grid.slope_row(1, b, c))
            put_pair(grid, (a, b, c), point_refs, pair_refs, weight)
    for place, cell in enumerate(grid.own_targets()):
        runs = grid.sources(cell, tuple(refs), grid.outer)
        before, after = load_four(column_ref, place), store_four(out_ref, place)
        add_force(left_ref, place, runs, refs, point_refs, pair_refs, before, after)


def last_force_kernel(own, stage, mid_ref, below_ref, above_ref, ghost_ref, ghost_edge_ref, ghost_point_ref, ghost_edge_point_ref, column_ref, left_ref, vel_ref, *out_refs):
    new_vel_ref, new_loc_ref, pair_ref, edge_pair_ref = out_refs
    grid = Grid(own)
    near = grid.cz + 2
    refs = {"gown": ghost_ref, "gedge": ghost_edge_ref}
    point_refs = {"gown": ghost_point_ref, "gedge": ghost_edge_point_ref}
    pair_refs = {"gown": pair_ref, "gedge": edge_pair_ref}
    for which in refs:
        for a, b, c in grid.cells_of(which, grid.outer):
            weight = row_of(below_ref if b == 0 else above_ref, int(a > 0) * near + c - 1)
            put_pair(grid, (a, b, c), point_refs, pair_refs, weight)
    for place, (a, b, c) in enumerate(grid.own_targets()):
        parts = []
        runs = grid.sources((a, b, c), tuple(refs), grid.outer)
        after = lambda chunk, total: parts.append(total)
        add_force(left_ref, place, runs, refs, point_refs, pair_refs, load_four(column_ref, place), after)
        flat = [across(jnp.concatenate([part[k] for part in parts], axis=0)) for k in range(4)]
        row = slice(place, place + 1)
        tile = mid_ref[a, b - 1, c - 2]
        point, _ = grid.placed(tile, a, b, c)
        scale = tile[3:4]
        present = jnp.where(scale > 0.5, -2.0, 0.0)
        kick = half_kick * jnp.where(scale > 1.05, 1.6, 1.0)
        for axis in range(3):
            force = present * (flat[axis] - point[axis : axis + 1] * flat[3])
            speed = vel_ref[axis, row, :] + kick * force
            if stage == "middle":
                speed = speed + kick * force
            new_vel_ref[axis, row, :] = speed
            if stage == "last":
                new_loc_ref[axis, row, :] = tile[axis : axis + 1]
            else:
                new_loc_ref[place, axis : axis + 1, :] = tile[axis : axis + 1] + time_step * speed
        if stage != "last":
            new_loc_ref[place, 3:4, :] = scale


def on_device(positions, velocities, species, counts):
    cx, cy, cz, slots = positions.shape[1:]
    own = (cx, cy, cz)
    cells = cx * cy * cz
    ex, near = cx + 2, cz + 2
    vmem = pl.BlockSpec(memory_space=pltpu.VMEM)
    flat_shape = jax.ShapeDtypeStruct((3, cells, slots), jnp.float32)
    sizes = {"own": ex * cy * cz, "edge": ex * cy * 2, "gown": 2 * ex * cz, "gedge": 2 * ex * 2}

    def block(which):
        return jax.ShapeDtypeStruct((48, sizes[which] * slots), jnp.bfloat16)

    def points(which):
        return jax.ShapeDtypeStruct((8, sizes[which] * slots), jnp.float32)

    def sums(*count):
        return jax.ShapeDtypeStruct((*count, slots, slots), jnp.float32)

    def rows(count):
        return jax.ShapeDtypeStruct((count, slots), jnp.float32)

    def lefts(count):
        return jax.ShapeDtypeStruct((count, slots, 48), jnp.bfloat16)

    def call(kernel, operands, out_shape, pairs, scratch=()):
        return pl.pallas_call(
            kernel,
            out_shape=out_shape,
            in_specs=[vmem] * len(operands),
            out_specs=[vmem] * len(out_shape),
            scratch_shapes=[pltpu.VMEM(item.shape, item.dtype) for item in scratch],
            compiler_params=pltpu.CompilerParams(vmem_limit_bytes=GRANT),
            cost_estimate=pl.CostEstimate(
                flops=pairs * slots * slots * 50, bytes_accessed=pairs * slots * slots * 4, transcendentals=0
            ),
        )(*operands)

    def evaluate(location, velocity, stage):
        mid = ring_halo(location, "gx", 0, 1)
        mid_below, mid_above = neighbours(mid, "gy", 1, 1)
        low, high = neighbours(mid, "gz", 2, 2)
        inner, part, point, ghost, ghost_point, left = call(
            functools.partial(inner_density_kernel, own),
            [mid, mid_below, mid_above],
            [sums(cells), block("own"), points("own"), block("gown"), points("gown"), lefts(cells)],
            cells * 18,
        )
        tall, inner = lax.optimization_barrier((jnp.concatenate([low, high], axis=2), inner))
        below, above = neighbours(tall, "gy", 1, 1)
        own_sum, edge_sum, edge, edge_point, edge_left = call(
            functools.partial(outer_density_kernel, own),
            [low, high, inner, part, ghost, left],
            [sums(cells), sums(cx * cy * 2), block("edge"), points("edge"), lefts(cx * cy * 2)],
            cells * 27,
            [block("edge")],
        )
        slopes, weights, ghost_edge, ghost_edge_point = call(
            functools.partial(last_density_kernel, own),
            [mid, low, high, below, above, own_sum, edge_sum, left, edge_left],
            [rows(cx * cy * near), rows(cx * cy * near), block("gedge"), points("gedge")],
            cells * 9,
            [block("gedge")],
        )
        weights = weights.reshape(cx, cy, near, slots)
        side_below, side_above = neighbours(weights, "gx", 0, 1)
        weight_below, weight_above = neighbours(weights, "gy", 1, 1)
        column, left = call(
            functools.partial(column_force_kernel, own),
            [
                mid,
                slopes,
                weights.reshape(cx * cy * near, slots),
                weight_below.reshape(cx * near, slots),
                weight_above.reshape(cx * near, slots),
                *(part, edge, ghost, ghost_edge),
                *(point, edge_point, ghost_point, ghost_edge_point),
            ],
            [sums(4, cells), lefts(cells)],
            cells * 9,
            [block(which) for which in SETS],
        )
        sides, column = lax.optimization_barrier((jnp.concatenate([side_below, side_above], axis=0), column))
        corner_below, corner_above = neighbours(sides, "gy", 1, 1)
        (column,) = call(
            functools.partial(side_force_kernel, own),
            [
                side_below.reshape(cy * near, slots),
                side_above.reshape(cy * near, slots),
                *(part, edge, point, edge_point, column, left),
            ],
            [sums(4, cells)],
            cells * 12,
            [block("own"), block("edge")],
        )
        moved = flat_shape if stage == "last" else jax.ShapeDtypeStruct((cells, 4, slots), jnp.float32)
        return call(
            functools.partial(last_force_kernel, own, stage),
            [
                mid,
                corner_below.reshape(2 * near, slots),
                corner_above.reshape(2 * near, slots),
                *(ghost, ghost_edge, ghost_point, ghost_edge_point, column, left, velocity),
            ],
            [flat_shape, moved],
            cells * 6,
            [block("gown"), block("gedge")],
        )

    arrays = [pltpu.with_memory_space_constraint(x, pltpu.HBM) for x in (positions, velocities, species, counts)]
    location, velocity = pl.pallas_call(
        prepare_kernel,
        out_shape=[jax.ShapeDtypeStruct((cx, cy, cz, 4, slots), jnp.float32), flat_shape],
        in_specs=[pl.BlockSpec(memory_space=pltpu.HBM)] * 4,
        out_specs=[vmem] * 2,
        scratch_shapes=[pltpu.VMEM(array.shape, array.dtype) for array in arrays] + [pltpu.SemaphoreType.DMA((4,))],
        compiler_params=pltpu.CompilerParams(vmem_limit_bytes=GRANT),
        name="prepare",
    )(*arrays)
    for stage in ("first", "middle", "last"):
        velocity, moved = evaluate(location.reshape(cx, cy, cz, 4, slots), velocity, stage)
        location = moved
    new_positions = moved
    return new_positions.reshape(positions.shape), velocity.reshape(positions.shape)


def solution(mesh):
    return jax.shard_map(
        on_device,
        mesh=mesh,
        in_specs=(
            P(None, "gx", "gy", "gz", None),
            P(None, "gx", "gy", "gz", None),
            P("gx", "gy", "gz", None),
            P("gx", "gy", "gz"),
        ),
        out_specs=(P(None, "gx", "gy", "gz", None), P(None, "gx", "gy", "gz", None)),
        check_vma=False,
    )
```

```python
import functools

import jax
import jax.numpy as jnp
from jax import lax
from jax.experimental import pallas as pl
from jax.experimental.pallas import tpu as pltpu
from jax.sharding import PartitionSpec as P


time_step = 0.05
half_kick = 0.5 * time_step
LANES = 128
GRANT = 8 * 1024 * 1024
ROOT = 1.3 ** (1.0 / 3.0)
STEPS = (-1, 0, 1)
SETS = ("own", "edge", "gown", "gedge")


def neighbours(cells, axis, dim, width, even=None):
    count = lax.axis_size(axis)
    size = cells.shape[dim]
    head = lax.slice_in_dim(cells, 0, width, axis=dim)
    tail = lax.slice_in_dim(cells, size - width, size, axis=dim)
    if count == 1:
        return tail, head
    if count == 2 and size == 2 * width:
        other = lax.ppermute(cells, axis, [(0, 1), (1, 0)])
        return (
            lax.slice_in_dim(other, width, size, axis=dim),
            lax.slice_in_dim(other, 0, width, axis=dim),
        )
    if count % 2:
        below = lax.ppermute(tail, axis, [(i, (i + 1) % count) for i in range(count)])
        above = lax.ppermute(head, axis, [((i + 1) % count, i) for i in range(count)])
        return below, above
    even = lax.axis_index(axis) % 2 == 0 if even is None else even
    first, second = (cells, cells) if size == width else (jnp.where(even, tail, head), jnp.where(even, head, tail))
    first = lax.ppermute(first, axis, [(i, i ^ 1) for i in range(count)])
    second = lax.ppermute(second, axis, [(i, (i - 1 if i % 2 == 0 else i + 1) % count) for i in range(count)])
    return jnp.where(even, second, first), jnp.where(even, first, second)


def ring_halo(cells, axis, dim, width, even=None):
    below, above = neighbours(cells, axis, dim, width, even)
    return jnp.concatenate([below, cells, above], axis=dim)


def split3(value):
    high = value.astype(jnp.bfloat16).astype(jnp.float32)
    rest = value - high
    middle = rest.astype(jnp.bfloat16).astype(jnp.float32)
    return high, middle, rest - middle


def partner_block(row):
    high, middle, low = split3(row)
    first = jnp.concatenate([high, middle], axis=0).astype(jnp.bfloat16)
    last = jnp.concatenate([low, high], axis=0).astype(jnp.bfloat16)
    return jnp.concatenate([first, first, last], axis=0)


def target_block(row):
    high, middle, low = split3(row)
    stacked = jnp.concatenate([high, high, middle, middle, high, low], axis=0)
    return jnp.transpose(stacked).astype(jnp.bfloat16)


class Grid:
    def __init__(self, own):
        self.cx, self.cy, self.cz = own
        self.ex, self.ey, self.ez = own[0] + 2, own[1] + 2, own[2] + 4
        row = lax.broadcasted_iota(jnp.int32, (8, LANES), 0)
        self.row = row
        self.masks = [(row == k).astype(jnp.float32) for k in range(7)]
        self.spatial = self.masks[0] + self.masks[1] + self.masks[2]
        self.inner = range(1, self.cx + 1)
        self.outer = (0, self.ex - 1)

    def own_targets(self):
        return [(a, b, c) for a in self.inner for b in range(1, self.cy + 1) for c in range(2, self.cz + 2)]

    def edge_targets(self):
        return [(a, b, c) for a in self.inner for b in range(1, self.cy + 1) for c in (1, self.cz + 2)]

    def slope_row(self, a, b, c):
        return ((a - 1) * self.cy + b - 1) * (self.cz + 2) + c - 1

    def place(self, a, b, c):
        if c in (0, self.ez - 1):
            which, layer = "far", int(c > 0)
        elif c in (1, self.ez - 2):
            which, layer = "edge", int(c > 1)
        else:
            which, layer = "own", c - 2
        if 1 <= b <= self.cy:
            return which, (layer * self.ex + a) * self.cy + b - 1
        layers = self.cz if which == "own" else 2
        column = self.outer.index(a) if a in self.outer else a + 1
        return "g" + which, (int(b > 0) * layers + layer) * self.ex + column

    def cells_of(self, which, columns=None):
        columns = range(self.ex) if columns is None else columns
        rows = (0, self.ey - 1) if which[0] == "g" else range(1, self.cy + 1)
        layers = {"n": range(2, self.cz + 2), "e": (1, self.ez - 2), "r": (0, self.ez - 1)}[
            "n" if which.endswith("own") else "e" if which.endswith("edge") else "r"
        ]
        return [(a, b, c) for c in layers for a in columns for b in rows]

    def sources(self, target, sets, columns=None):
        found = {}
        for p in STEPS:
            for q in STEPS:
                for r in STEPS:
                    a, b, c = target[0] + p, target[1] + q, target[2] + r
                    which, index = self.place(a, b, c)
                    if which in sets and (columns is None or a in columns):
                        found.setdefault(which, []).append((index, p == q == r == 0))
        runs = []
        for which in sets:
            entries = sorted(found.get(which, []))
            while entries:
                length = 1
                while length < len(entries) and entries[length][0] == entries[0][0] + length:
                    length += 1
                count = min(length, 2 if length % 2 == 0 else 3)
                same = [k for k in range(count) if entries[k][1]]
                runs.append((which, entries[0][0], count, same[0] if same else -1))
                entries = entries[count:]
        return runs

    def placed(self, tile, a, b, c):
        m = self.masks
        shift = (
            (a + 0.5 - 0.5 * self.ex) * m[0]
            + (b + 0.5 - 0.5 * self.ey) * m[1]
            + (m[4] + (c + 0.5 - 0.5 * self.ez) * m[2])
        )
        point = jnp.concatenate([tile, jnp.zeros((4, LANES), jnp.float32)], axis=0)
        point = point * self.spatial + shift
        return point, jnp.sum(point * point, axis=0, keepdims=True)

    def put_partner(self, tile, cell, refs, point_refs=None):
        which, index = self.place(*cell)
        lanes = slice(index * LANES, (index + 1) * LANES)
        point, bulk = self.placed(tile, *cell)
        scale = tile[3:4]
        refs[which][:, lanes] = partner_block(jnp.where(self.row == 3, 1.0 - bulk, point) * scale)
        if point_refs is not None:
            strength = jnp.where(scale > 1.05, 0.4 / ROOT, 0.3)
            point_refs[which][:, lanes] = jnp.where(
                self.row == 3, strength, jnp.where(self.row == 4, scale, point)
            )

    def target(self, tile, a, b, c):
        point, bulk = self.placed(tile, a, b, c)
        twice = jnp.where(self.row == 4, 2.0 - bulk, 2.0 * point)
        return twice + self.masks[3]


def across(total):
    return jnp.sum(jnp.transpose(total), axis=0, keepdims=True)


def add_density(left_ref, place, runs, refs, before, after):
    rows = 128
    for start in range(0, LANES, rows):
        chunk = slice(start, start + rows)
        total = before(chunk)
        for which, first, count, same in runs:
            near = jnp.dot(
                left_ref[place, chunk, :],
                refs[which][:, first * LANES : (first + count) * LANES],
                preferred_element_type=jnp.float32,
            )
            for k in range(count):
                part = jnp.maximum(near[:, k * LANES : (k + 1) * LANES], 0.0)
                if k == same:
                    i = lax.broadcasted_iota(jnp.int32, (rows, LANES), 0)
                    j = lax.broadcasted_iota(jnp.int32, (rows, LANES), 1)
                    part = jnp.where(i + start == j, 0.0, part)
                cube = part * part * part
                total = cube if total is None else total + cube
        after(chunk, total)


def store_to(ref, place):
    def after(chunk, total):
        ref[place, chunk, :] = total

    return after


def nothing(chunk):
    return None


def prepare_kernel(pos_hbm, vel_hbm, species_hbm, counts_hbm, loc_ref, out_ref, pos_ref, vel_ref, species_ref, counts_ref, arrived):
    copies = [
        pltpu.make_async_copy(source, target, arrived.at[k])
        for k, (source, target) in enumerate(
            ((pos_hbm, pos_ref), (vel_hbm, vel_ref), (species_hbm, species_ref), (counts_hbm, counts_ref))
        )
    ]
    for copy in copies:
        copy.start()
    for copy in copies:
        copy.wait()
    cx, cy, cz = pos_ref.shape[1:4]
    slot = lax.broadcasted_iota(jnp.int32, (1, LANES), 1)
    for a in range(cx):
        for b in range(cy):
            for c in range(cz):
                place = (a * cy + b) * cz + c
                one = slice(c, c + 1)
                for axis in range(3):
                    loc_ref[a, b, c, axis : axis + 1, :] = pos_ref[axis, a, b, one, :]
                    out_ref[axis, place : place + 1, :] = vel_ref[axis, a, b, one, :]
                kind = jnp.where(species_ref[a, b, one, :] == 1, ROOT, 1.0)
                count = jnp.broadcast_to(counts_ref[a, b : b + 1, one], (1, LANES))
                loc_ref[a, b, c, 3:4, :] = jnp.where(slot < count, kind, 0.0)


def inner_density_kernel(own, mid_ref, below_ref, above_ref, sum_ref, part_ref, point_ref, ghost_ref, ghost_point_ref, left_ref):
    grid = Grid(own)
    refs = {"own": part_ref, "gown": ghost_ref}
    point_refs = {"own": point_ref, "gown": ghost_point_ref}
    for a, b, c in grid.cells_of("own"):
        grid.put_partner(mid_ref[a, b - 1, c - 2], (a, b, c), refs, point_refs)
    for a, b, c in grid.cells_of("gown"):
        tile = (below_ref if b == 0 else above_ref)[a, 0, c - 2]
        grid.put_partner(tile, (a, b, c), refs, point_refs)
    for place, (a, b, c) in enumerate(grid.own_targets()):
        left_ref[place] = target_block(grid.target(mid_ref[a, b - 1, c - 2], a, b, c))
        runs = grid.sources((a, b, c), ("own", "gown"))
        add_density(left_ref, place, runs, refs, nothing, store_to(sum_ref, place))


def outer_density_kernel(own, low_ref, high_ref, inner_ref, part_ref, ghost_ref, left_ref, own_sum_ref, edge_sum_ref, edge_ref, edge_point_ref, edge_left_ref, far_ref):
    grid = Grid(own)
    refs = {"own": part_ref, "gown": ghost_ref, "edge": edge_ref, "far": far_ref}

    def tile_of(a, b, c):
        return low_ref[a, b - 1, c] if c < 2 else high_ref[a, b - 1, c - grid.cz - 2]

    for cell in grid.cells_of("edge"):
        grid.put_partner(tile_of(*cell), cell, refs, {"edge": edge_point_ref})
    for cell in grid.cells_of("far"):
        grid.put_partner(tile_of(*cell), cell, refs)
    for place, cell in enumerate(grid.edge_targets()):
        edge_left_ref[place] = target_block(grid.target(tile_of(*cell), *cell))
        runs = grid.sources(cell, ("own", "gown", "edge", "far"))
        add_density(edge_left_ref, place, runs, refs, nothing, store_to(edge_sum_ref, place))
    for place, cell in enumerate(grid.own_targets()):
        runs = grid.sources(cell, ("edge",))
        before = lambda chunk, place=place: inner_ref[place, chunk, :]
        add_density(left_ref, place, runs, refs, before, store_to(own_sum_ref, place))


def last_density_kernel(own, mid_ref, low_ref, high_ref, below_ref, above_ref, own_sum_ref, edge_sum_ref, left_ref, edge_left_ref, slope_ref, weight_ref, ghost_ref, ghost_point_ref, far_ref):
    grid = Grid(own)
    refs = {"gedge": ghost_ref, "gfar": far_ref}
    for which in ("gedge", "gfar"):
        for a, b, c in grid.cells_of(which):
            tile = (below_ref if b == 0 else above_ref)[a, 0, c if c < 2 else c - grid.cz]
            grid.put_partner(tile, (a, b, c), refs, {"gedge": ghost_point_ref} if which == "gedge" else None)
    groups = ((grid.own_targets(), own_sum_ref, left_ref), (grid.edge_targets(), edge_sum_ref, edge_left_ref))
    for targets, sum_ref, rows_ref in groups:
        for place, (a, b, c) in enumerate(targets):
            if c < 2:
                tile = low_ref[a, b - 1, c]
            elif c >= grid.cz + 2:
                tile = high_ref[a, b - 1, c - grid.cz - 2]
            else:
                tile = mid_ref[a, b - 1, c - 2]
            runs = grid.sources((a, b, c), ("gedge", "gfar"))
            parts = []
            before = lambda chunk, place=place, sum_ref=sum_ref: sum_ref[place, chunk, :]
            add_density(rows_ref, place, runs, refs, before, lambda chunk, total: parts.append(total))
            density = across(jnp.concatenate(parts, axis=0))
            scale = tile[3:4]
            slope = jnp.where(scale > 0.5, -0.5, 0.0) / jnp.sqrt(density + 1.0)
            where = grid.slope_row(a, b, c)
            slope_ref[where : where + 1, :] = slope
            weight_ref[where : where + 1, :] = slope * jnp.where(scale > 1.05, 0.75 / (ROOT * ROOT), 0.75)


def put_pair(grid, cell, point_refs, pair_refs, weight):
    which, index = grid.place(*cell)
    lanes = slice(index * LANES, (index + 1) * LANES)
    scale = point_refs[which][4:5, lanes]
    row = jnp.where(grid.row == 5, 0.75 * scale, jnp.where(grid.row == 6, weight, 0.0))
    high = row.astype(jnp.bfloat16).astype(jnp.float32)
    first = jnp.concatenate([high, row - high], axis=0).astype(jnp.bfloat16)
    last = jnp.concatenate([jnp.zeros((8, LANES), jnp.float32), high], axis=0).astype(jnp.bfloat16)
    pair_refs[which][:, lanes] = jnp.concatenate([first, first, last], axis=0)


def add_force(left_ref, place, runs, refs, point_refs, pair_refs, before, after):
    rows = 128
    for start in range(0, LANES, rows):
        chunk = slice(start, start + rows)
        total = before(chunk)
        left = left_ref[place, chunk, :]
        for which, first, count, _ in runs:
            span = slice(first * LANES, (first + count) * LANES)
            near = jnp.dot(left, refs[which][:, span], preferred_element_type=jnp.float32)
            kappa = jnp.dot(left, pair_refs[which][:, span], preferred_element_type=jnp.float32)
            value_ref = point_refs[which]
            for k in range(count):
                part = slice(k * LANES, (k + 1) * LANES)
                lanes = slice((first + k) * LANES, (first + k + 1) * LANES)
                s = jnp.maximum(near[:, part], 0.0)
                w = s * (value_ref[3:4, lanes] + s * kappa[:, part])
                new = [w * value_ref[axis : axis + 1, lanes] for axis in range(3)] + [w]
                total = new if total is None else [old + more for old, more in zip(total, new)]
        after(chunk, total)


def store_four(ref, place):
    def after(chunk, total):
        for k in range(4):
            ref[k, place, chunk, :] = total[k]

    return after


def load_four(ref, place):
    def before(chunk):
        return [ref[k, place, chunk, :] for k in range(4)]

    return before


def row_of(ref, index):
    return ref[index : index + 1, :]


def column_force_kernel(own, *all_refs):
    mid_ref, slope_ref, weight_ref, below_ref, above_ref = all_refs[:5]
    refs = dict(zip(SETS, all_refs[5:9]))
    point_refs = dict(zip(SETS, all_refs[9:13]))
    out_ref, left_ref = all_refs[13:15]
    pair_refs = dict(zip(SETS, all_refs[15:]))
    grid = Grid(own)
    m = grid.masks
    near = grid.cz + 2
    for which in SETS:
        for a, b, c in grid.cells_of(which, grid.inner):
            if which[0] == "g":
                weight = row_of(below_ref if b == 0 else above_ref, (a - 1) * near + c - 1)
            else:
                weight = row_of(weight_ref, grid.slope_row(a, b, c))
            put_pair(grid, (a, b, c), point_refs, pair_refs, weight)
    for place, (a, b, c) in enumerate(grid.own_targets()):
        tile = mid_ref[a, b - 1, c - 2]
        solute = tile[3:4] > 1.05
        left_ref[place] = target_block(
            grid.target(tile, a, b, c) * jnp.where(solute, 0.8, 0.6)
            + row_of(slope_ref, grid.slope_row(a, b, c)) * jnp.where(solute, 1.0 / 0.16, 1.0 / 0.09) * m[5]
            + jnp.where(solute, 1.3 / 0.16, 1.0 / 0.09) * m[6]
        )
        runs = grid.sources((a, b, c), SETS, grid.inner)
        add_force(left_ref, place, runs, refs, point_refs, pair_refs, nothing, store_four(out_ref, place))


def side_force_kernel(own, below_ref, above_ref, part_ref, edge_ref, point_ref, edge_point_ref, column_ref, left_ref, out_ref, pair_ref, edge_pair_ref):
    grid = Grid(own)
    refs = {"own": part_ref, "edge": edge_ref}
    point_refs = {"own": point_ref, "edge": edge_point_ref}
    pair_refs = {"own": pair_ref, "edge": edge_pair_ref}
    for which in refs:
        for a, b, c in grid.cells_of(which, grid.outer):
            weight = row_of(below_ref if a == 0 else above_ref, grid.slope_row(1, b, c))
            put_pair(grid, (a, b, c), point_refs, pair_refs, weight)
    for place, cell in enumerate(grid.own_targets()):
        runs = grid.sources(cell, tuple(refs), grid.outer)
        before, after = load_four(column_ref, place), store_four(out_ref, place)
        add_force(left_ref, place, runs, refs, point_refs, pair_refs, before, after)


def last_force_kernel(own, stage, mid_ref, below_ref, above_ref, ghost_ref, ghost_edge_ref, ghost_point_ref, ghost_edge_point_ref, column_ref, left_ref, vel_ref, *out_refs):
    new_vel_ref, new_loc_ref, pair_ref, edge_pair_ref = out_refs
    grid = Grid(own)
    near = grid.cz + 2
    refs = {"gown": ghost_ref, "gedge": ghost_edge_ref}
    point_refs = {"gown": ghost_point_ref, "gedge": ghost_edge_point_ref}
    pair_refs = {"gown": pair_ref, "gedge": edge_pair_ref}
    for which in refs:
        for a, b, c in grid.cells_of(which, grid.outer):
            weight = row_of(below_ref if b == 0 else above_ref, int(a > 0) * near + c - 1)
            put_pair(grid, (a, b, c), point_refs, pair_refs, weight)
    for place, (a, b, c) in enumerate(grid.own_targets()):
        parts = []
        runs = grid.sources((a, b, c), tuple(refs), grid.outer)
        after = lambda chunk, total: parts.append(total)
        add_force(left_ref, place, runs, refs, point_refs, pair_refs, load_four(column_ref, place), after)
        flat = [across(jnp.concatenate([part[k] for part in parts], axis=0)) for k in range(4)]
        row = slice(place, place + 1)
        tile = mid_ref[a, b - 1, c - 2]
        point, _ = grid.placed(tile, a, b, c)
        scale = tile[3:4]
        present = jnp.where(scale > 0.5, -2.0, 0.0)
        kick = half_kick * jnp.where(scale > 1.05, 1.6, 1.0)
        for axis in range(3):
            force = present * (flat[axis] - point[axis : axis + 1] * flat[3])
            speed = vel_ref[axis, row, :] + kick * force
            if stage == "middle":
                speed = speed + kick * force
            new_vel_ref[axis, row, :] = speed
            if stage == "last":
                new_loc_ref[axis, row, :] = tile[axis : axis + 1]
            else:
                new_loc_ref[place, axis : axis + 1, :] = tile[axis : axis + 1] + time_step * speed
        if stage != "last":
            new_loc_ref[place, 3:4, :] = scale


def on_device(positions, velocities, species, counts):
    cx, cy, cz, slots = positions.shape[1:]
    own = (cx, cy, cz)
    cells = cx * cy * cz
    ex, near = cx + 2, cz + 2
    vmem = pl.BlockSpec(memory_space=pltpu.VMEM)
    flat_shape = jax.ShapeDtypeStruct((3, cells, slots), jnp.float32)
    sizes = {"own": ex * cy * cz, "edge": ex * cy * 2, "gown": 2 * ex * cz, "gedge": 2 * ex * 2}

    def block(which):
        return jax.ShapeDtypeStruct((48, sizes[which] * slots), jnp.bfloat16)

    def points(which):
        return jax.ShapeDtypeStruct((8, sizes[which] * slots), jnp.float32)

    def sums(*count):
        return jax.ShapeDtypeStruct((*count, slots, slots), jnp.float32)

    def rows(count):
        return jax.ShapeDtypeStruct((count, slots), jnp.float32)

    def lefts(count):
        return jax.ShapeDtypeStruct((count, slots, 48), jnp.bfloat16)

    def call(kernel, operands, out_shape, pairs, scratch=()):
        return pl.pallas_call(
            kernel,
            out_shape=out_shape,
            in_specs=[vmem] * len(operands),
            out_specs=[vmem] * len(out_shape),
            scratch_shapes=[pltpu.VMEM(item.shape, item.dtype) for item in scratch],
            compiler_params=pltpu.CompilerParams(vmem_limit_bytes=GRANT),
            cost_estimate=pl.CostEstimate(
                flops=pairs * slots * slots * 50, bytes_accessed=pairs * slots * slots * 4, transcendentals=0
            ),
        )(*operands)

    even = {axis: lax.optimization_barrier(lax.axis_index(axis) % 2 == 0) for axis in ("gx", "gz")}

    def evaluate(location, velocity, stage):
        mid = ring_halo(location, "gx", 0, 1, even["gx"])
        mid_below, mid_above = neighbours(mid, "gy", 1, 1)
        low, high = neighbours(mid, "gz", 2, 2, even["gz"])
        inner, part, point, ghost, ghost_point, left = call(
            functools.partial(inner_density_kernel, own),
            [mid, mid_below, mid_above],
            [sums(cells), block("own"), points("own"), block("gown"), points("gown"), lefts(cells)],
            cells * 18,
        )
        tall, inner = lax.optimization_barrier((jnp.concatenate([low, high], axis=2), inner))
        below, above = neighbours(tall, "gy", 1, 1)
        own_sum, edge_sum, edge, edge_point, edge_left = call(
            functools.partial(outer_density_kernel, own),
            [low, high, inner, part, ghost, left],
            [sums(cells), sums(cx * cy * 2), block("edge"), points("edge"), lefts(cx * cy * 2)],
            cells * 27,
            [block("edge")],
        )
        slopes, weights, ghost_edge, ghost_edge_point = call(
            functools.partial(last_density_kernel, own),
            [mid, low, high, below, above, own_sum, edge_sum, left, edge_left],
            [rows(cx * cy * near), rows(cx * cy * near), block("gedge"), points("gedge")],
            cells * 9,
            [block("gedge")],
        )
        weights = weights.reshape(cx, cy, near, slots)
        side_below, side_above = neighbours(weights, "gx", 0, 1, even["gx"])
        weight_below, weight_above = neighbours(weights, "gy", 1, 1)
        column, left = call(
            functools.partial(column_force_kernel, own),
            [
                mid,
                slopes,
                weights.reshape(cx * cy * near, slots),
                weight_below.reshape(cx * near, slots),
                weight_above.reshape(cx * near, slots),
                *(part, edge, ghost, ghost_edge),
                *(point, edge_point, ghost_point, ghost_edge_point),
            ],
            [sums(4, cells), lefts(cells)],
            cells * 9,
            [block(which) for which in SETS],
        )
        sides, column = lax.optimization_barrier((jnp.concatenate([side_below, side_above], axis=0), column))
        corner_below, corner_above = neighbours(sides, "gy", 1, 1)
        (column,) = call(
            functools.partial(side_force_kernel, own),
            [
                side_below.reshape(cy * near, slots),
                side_above.reshape(cy * near, slots),
                *(part, edge, point, edge_point, column, left),
            ],
            [sums(4, cells)],
            cells * 12,
            [block("own"), block("edge")],
        )
        moved = flat_shape if stage == "last" else jax.ShapeDtypeStruct((cells, 4, slots), jnp.float32)
        return call(
            functools.partial(last_force_kernel, own, stage),
            [
                mid,
                corner_below.reshape(2 * near, slots),
                corner_above.reshape(2 * near, slots),
                *(ghost, ghost_edge, ghost_point, ghost_edge_point, column, left, velocity),
            ],
            [flat_shape, moved],
            cells * 6,
            [block("gown"), block("gedge")],
        )

    arrays = [pltpu.with_memory_space_constraint(x, pltpu.HBM) for x in (positions, velocities, species, counts)]
    location, velocity = pl.pallas_call(
        prepare_kernel,
        out_shape=[jax.ShapeDtypeStruct((cx, cy, cz, 4, slots), jnp.float32), flat_shape],
        in_specs=[pl.BlockSpec(memory_space=pltpu.HBM)] * 4,
        out_specs=[vmem] * 2,
        scratch_shapes=[pltpu.VMEM(array.shape, array.dtype) for array in arrays] + [pltpu.SemaphoreType.DMA((4,))],
        compiler_params=pltpu.CompilerParams(vmem_limit_bytes=GRANT),
        name="prepare",
    )(*arrays)
    for stage in ("first", "middle", "last"):
        velocity, moved = evaluate(location.reshape(cx, cy, cz, 4, slots), velocity, stage)
        location = moved
    new_positions = moved
    return new_positions.reshape(positions.shape), velocity.reshape(positions.shape)


def solution(mesh):
    return jax.shard_map(
        on_device,
        mesh=mesh,
        in_specs=(
            P(None, "gx", "gy", "gz", None),
            P(None, "gx", "gy", "gz", None),
            P("gx", "gy", "gz", None),
            P("gx", "gy", "gz"),
        ),
        out_specs=(P(None, "gx", "gy", "gz", None), P(None, "gx", "gy", "gz", None)),
        check_vma=False,
    )
```

```python
import functools

import jax
import jax.numpy as jnp
from jax import lax
from jax.experimental import pallas as pl
from jax.experimental.pallas import tpu as pltpu
from jax.sharding import PartitionSpec as P


time_step = 0.05
half_kick = 0.5 * time_step
LANES = 128
GRANT = 8 * 1024 * 1024
ROOT = 1.3 ** (1.0 / 3.0)
STEPS = (-1, 0, 1)
SETS = ("own", "edge", "gown", "gedge")


def neighbours(cells, axis, dim, width, even=None):
    count = lax.axis_size(axis)
    size = cells.shape[dim]
    head = lax.slice_in_dim(cells, 0, width, axis=dim)
    tail = lax.slice_in_dim(cells, size - width, size, axis=dim)
    if count == 1:
        return tail, head
    if count == 2 and size == 2 * width:
        other = lax.ppermute(cells, axis, [(0, 1), (1, 0)])
        return (
            lax.slice_in_dim(other, width, size, axis=dim),
            lax.slice_in_dim(other, 0, width, axis=dim),
        )
    if even is None or count % 2:
        below = lax.ppermute(tail, axis, [(i, (i + 1) % count) for i in range(count)])
        above = lax.ppermute(head, axis, [((i + 1) % count, i) for i in range(count)])
        return below, above
    first, second = (cells, cells) if size == width else (jnp.where(even, tail, head), jnp.where(even, head, tail))
    first = lax.ppermute(first, axis, [(i, i ^ 1) for i in range(count)])
    second = lax.ppermute(second, axis, [(i, (i - 1 if i % 2 == 0 else i + 1) % count) for i in range(count)])
    return jnp.where(even, second, first), jnp.where(even, first, second)


def ring_halo(cells, axis, dim, width, even=None):
    below, above = neighbours(cells, axis, dim, width, even)
    return jnp.concatenate([below, cells, above], axis=dim)


def split3(value):
    high = value.astype(jnp.bfloat16).astype(jnp.float32)
    rest = value - high
    middle = rest.astype(jnp.bfloat16).astype(jnp.float32)
    return high, middle, rest - middle


def partner_block(row):
    high, middle, low = split3(row)
    first = jnp.concatenate([high, middle], axis=0).astype(jnp.bfloat16)
    last = jnp.concatenate([low, high], axis=0).astype(jnp.bfloat16)
    return jnp.concatenate([first, first, last], axis=0)


def target_block(row):
    high, middle, low = split3(row)
    stacked = jnp.concatenate([high, high, middle, middle, high, low], axis=0)
    return jnp.transpose(stacked).astype(jnp.bfloat16)


class Grid:
    def __init__(self, own):
        self.cx, self.cy, self.cz = own
        self.ex, self.ey, self.ez = own[0] + 2, own[1] + 2, own[2] + 4
        row = lax.broadcasted_iota(jnp.int32, (8, LANES), 0)
        self.row = row
        self.masks = [(row == k).astype(jnp.float32) for k in range(7)]
        self.spatial = self.masks[0] + self.masks[1] + self.masks[2]
        self.inner = range(1, self.cx + 1)
        self.outer = (0, self.ex - 1)

    def own_targets(self):
        return [(a, b, c) for a in self.inner for b in range(1, self.cy + 1) for c in range(2, self.cz + 2)]

    def edge_targets(self):
        return [(a, b, c) for a in self.inner for b in range(1, self.cy + 1) for c in (1, self.cz + 2)]

    def slope_row(self, a, b, c):
        return ((a - 1) * self.cy + b - 1) * (self.cz + 2) + c - 1

    def place(self, a, b, c):
        if c in (0, self.ez - 1):
            which, layer = "far", int(c > 0)
        elif c in (1, self.ez - 2):
            which, layer = "edge", int(c > 1)
        else:
            which, layer = "own", c - 2
        if 1 <= b <= self.cy:
            return which, (layer * self.ex + a) * self.cy + b - 1
        layers = self.cz if which == "own" else 2
        column = self.outer.index(a) if a in self.outer else a + 1
        return "g" + which, (int(b > 0) * layers + layer) * self.ex + column

    def cells_of(self, which, columns=None):
        columns = range(self.ex) if columns is None else columns
        rows = (0, self.ey - 1) if which[0] == "g" else range(1, self.cy + 1)
        layers = {"n": range(2, self.cz + 2), "e": (1, self.ez - 2), "r": (0, self.ez - 1)}[
            "n" if which.endswith("own") else "e" if which.endswith("edge") else "r"
        ]
        return [(a, b, c) for c in layers for a in columns for b in rows]

    def sources(self, target, sets, columns=None):
        found = {}
        for p in STEPS:
            for q in STEPS:
                for r in STEPS:
                    a, b, c = target[0] + p, target[1] + q, target[2] + r
                    which, index = self.place(a, b, c)
                    if which in sets and (columns is None or a in columns):
                        found.setdefault(which, []).append((index, p == q == r == 0))
        runs = []
        for which in sets:
            entries = sorted(found.get(which, []))
            while entries:
                length = 1
                while length < len(entries) and entries[length][0] == entries[0][0] + length:
                    length += 1
                count = min(length, 2 if length % 2 == 0 else 3)
                same = [k for k in range(count) if entries[k][1]]
                runs.append((which, entries[0][0], count, same[0] if same else -1))
                entries = entries[count:]
        return runs

    def placed(self, tile, a, b, c):
        m = self.masks
        shift = (
            (a + 0.5 - 0.5 * self.ex) * m[0]
            + (b + 0.5 - 0.5 * self.ey) * m[1]
            + (m[4] + (c + 0.5 - 0.5 * self.ez) * m[2])
        )
        point = jnp.concatenate([tile, jnp.zeros((4, LANES), jnp.float32)], axis=0)
        point = point * self.spatial + shift
        return point, jnp.sum(point * point, axis=0, keepdims=True)

    def put_partner(self, tile, cell, refs, point_refs=None):
        which, index = self.place(*cell)
        lanes = slice(index * LANES, (index + 1) * LANES)
        point, bulk = self.placed(tile, *cell)
        scale = tile[3:4]
        refs[which][:, lanes] = partner_block(jnp.where(self.row == 3, 1.0 - bulk, point) * scale)
        if point_refs is not None:
            strength = jnp.where(scale > 1.05, 0.4 / ROOT, 0.3)
            point_refs[which][:, lanes] = jnp.where(
                self.row == 3, strength, jnp.where(self.row == 4, scale, point)
            )

    def target(self, tile, a, b, c):
        point, bulk = self.placed(tile, a, b, c)
        twice = jnp.where(self.row == 4, 2.0 - bulk, 2.0 * point)
        return twice + self.masks[3]


def across(total):
    return jnp.sum(jnp.transpose(total), axis=0, keepdims=True)


def add_density(left_ref, place, runs, refs, before, after):
    rows = 128
    for start in range(0, LANES, rows):
        chunk = slice(start, start + rows)
        total = before(chunk)
        for which, first, count, same in runs:
            near = jnp.dot(
                left_ref[place, chunk, :],
                refs[which][:, first * LANES : (first + count) * LANES],
                preferred_element_type=jnp.float32,
            )
            for k in range(count):
                part = jnp.maximum(near[:, k * LANES : (k + 1) * LANES], 0.0)
                if k == same:
                    i = lax.broadcasted_iota(jnp.int32, (rows, LANES), 0)
                    j = lax.broadcasted_iota(jnp.int32, (rows, LANES), 1)
                    part = jnp.where(i + start == j, 0.0, part)
                cube = part * part * part
                total = cube if total is None else total + cube
        after(chunk, total)


def store_to(ref, place):
    def after(chunk, total):
        ref[place, chunk, :] = total

    return after


def nothing(chunk):
    return None


def prepare_kernel(pos_hbm, vel_hbm, species_hbm, counts_hbm, loc_ref, out_ref, pos_ref, vel_ref, species_ref, counts_ref, arrived):
    copies = [
        pltpu.make_async_copy(source, target, arrived.at[k])
        for k, (source, target) in enumerate(
            ((pos_hbm, pos_ref), (vel_hbm, vel_ref), (species_hbm, species_ref), (counts_hbm, counts_ref))
        )
    ]
    for copy in copies:
        copy.start()
    for copy in copies:
        copy.wait()
    cx, cy, cz = pos_ref.shape[1:4]
    slot = lax.broadcasted_iota(jnp.int32, (1, LANES), 1)
    for a in range(cx):
        for b in range(cy):
            for c in range(cz):
                place = (a * cy + b) * cz + c
                one = slice(c, c + 1)
                for axis in range(3):
                    loc_ref[a, b, c, axis : axis + 1, :] = pos_ref[axis, a, b, one, :]
                    out_ref[axis, place : place + 1, :] = vel_ref[axis, a, b, one, :]
                kind = jnp.where(species_ref[a, b, one, :] == 1, ROOT, 1.0)
                count = jnp.broadcast_to(counts_ref[a, b : b + 1, one], (1, LANES))
                loc_ref[a, b, c, 3:4, :] = jnp.where(slot < count, kind, 0.0)


def inner_density_kernel(own, mid_ref, below_ref, above_ref, sum_ref, part_ref, point_ref, ghost_ref, ghost_point_ref, left_ref):
    grid = Grid(own)
    refs = {"own": part_ref, "gown": ghost_ref}
    point_refs = {"own": point_ref, "gown": ghost_point_ref}
    for a, b, c in grid.cells_of("own"):
        grid.put_partner(mid_ref[a, b - 1, c - 2], (a, b, c), refs, point_refs)
    for a, b, c in grid.cells_of("gown"):
        tile = (below_ref if b == 0 else above_ref)[a, 0, c - 2]
        grid.put_partner(tile, (a, b, c), refs, point_refs)
    for place, (a, b, c) in enumerate(grid.own_targets()):
        left_ref[place] = target_block(grid.target(mid_ref[a, b - 1, c - 2], a, b, c))
        runs = grid.sources((a, b, c), ("own", "gown"))
        add_density(left_ref, place, runs, refs, nothing, store_to(sum_ref, place))


def outer_density_kernel(own, low_ref, high_ref, inner_ref, part_ref, ghost_ref, left_ref, own_sum_ref, edge_sum_ref, edge_ref, edge_point_ref, edge_left_ref, far_ref):
    grid = Grid(own)
    refs = {"own": part_ref, "gown": ghost_ref, "edge": edge_ref, "far": far_ref}

    def tile_of(a, b, c):
        return low_ref[a, b - 1, c] if c < 2 else high_ref[a, b - 1, c - grid.cz - 2]

    for cell in grid.cells_of("edge"):
        grid.put_partner(tile_of(*cell), cell, refs, {"edge": edge_point_ref})
    for cell in grid.cells_of("far"):
        grid.put_partner(tile_of(*cell), cell, refs)
    for place, cell in enumerate(grid.edge_targets()):
        edge_left_ref[place] = target_block(grid.target(tile_of(*cell), *cell))
        runs = grid.sources(cell, ("own", "gown", "edge", "far"))
        add_density(edge_left_ref, place, runs, refs, nothing, store_to(edge_sum_ref, place))
    for place, cell in enumerate(grid.own_targets()):
        runs = grid.sources(cell, ("edge",))
        before = lambda chunk, place=place: inner_ref[place, chunk, :]
        add_density(left_ref, place, runs, refs, before, store_to(own_sum_ref, place))


def last_density_kernel(own, mid_ref, low_ref, high_ref, below_ref, above_ref, own_sum_ref, edge_sum_ref, left_ref, edge_left_ref, slope_ref, weight_ref, ghost_ref, ghost_point_ref, far_ref):
    grid = Grid(own)
    refs = {"gedge": ghost_ref, "gfar": far_ref}
    for which in ("gedge", "gfar"):
        for a, b, c in grid.cells_of(which):
            tile = (below_ref if b == 0 else above_ref)[a, 0, c if c < 2 else c - grid.cz]
            grid.put_partner(tile, (a, b, c), refs, {"gedge": ghost_point_ref} if which == "gedge" else None)
    groups = ((grid.own_targets(), own_sum_ref, left_ref), (grid.edge_targets(), edge_sum_ref, edge_left_ref))
    for targets, sum_ref, rows_ref in groups:
        for place, (a, b, c) in enumerate(targets):
            if c < 2:
                tile = low_ref[a, b - 1, c]
            elif c >= grid.cz + 2:
                tile = high_ref[a, b - 1, c - grid.cz - 2]
            else:
                tile = mid_ref[a, b - 1, c - 2]
            runs = grid.sources((a, b, c), ("gedge", "gfar"))
            parts = []
            before = lambda chunk, place=place, sum_ref=sum_ref: sum_ref[place, chunk, :]
            add_density(rows_ref, place, runs, refs, before, lambda chunk, total: parts.append(total))
            density = across(jnp.concatenate(parts, axis=0))
            scale = tile[3:4]
            slope = jnp.where(scale > 0.5, -0.5, 0.0) / jnp.sqrt(density + 1.0)
            where = grid.slope_row(a, b, c)
            slope_ref[where : where + 1, :] = slope
            weight_ref[where : where + 1, :] = slope * jnp.where(scale > 1.05, 0.75 / (ROOT * ROOT), 0.75)


def put_pair(grid, cell, point_refs, pair_refs, weight):
    which, index = grid.place(*cell)
    lanes = slice(index * LANES, (index + 1) * LANES)
    scale = point_refs[which][4:5, lanes]
    row = jnp.where(grid.row == 5, 0.75 * scale, jnp.where(grid.row == 6, weight, 0.0))
    high = row.astype(jnp.bfloat16).astype(jnp.float32)
    first = jnp.concatenate([high, row - high], axis=0).astype(jnp.bfloat16)
    last = jnp.concatenate([jnp.zeros((8, LANES), jnp.float32), high], axis=0).astype(jnp.bfloat16)
    pair_refs[which][:, lanes] = jnp.concatenate([first, first, last], axis=0)


def add_force(left_ref, place, runs, refs, point_refs, pair_refs, before, after):
    rows = 128
    for start in range(0, LANES, rows):
        chunk = slice(start, start + rows)
        total = before(chunk)
        left = left_ref[place, chunk, :]
        for which, first, count, _ in runs:
            span = slice(first * LANES, (first + count) * LANES)
            near = jnp.dot(left, refs[which][:, span], preferred_element_type=jnp.float32)
            kappa = jnp.dot(left, pair_refs[which][:, span], preferred_element_type=jnp.float32)
            value_ref = point_refs[which]
            for k in range(count):
                part = slice(k * LANES, (k + 1) * LANES)
                lanes = slice((first + k) * LANES, (first + k + 1) * LANES)
                s = jnp.maximum(near[:, part], 0.0)
                w = s * (value_ref[3:4, lanes] + s * kappa[:, part])
                new = [w * value_ref[axis : axis + 1, lanes] for axis in range(3)] + [w]
                total = new if total is None else [old + more for old, more in zip(total, new)]
        after(chunk, total)


def store_four(ref, place):
    def after(chunk, total):
        for k in range(4):
            ref[k, place, chunk, :] = total[k]

    return after


def load_four(ref, place):
    def before(chunk):
        return [ref[k, place, chunk, :] for k in range(4)]

    return before


def row_of(ref, index):
    return ref[index : index + 1, :]


def column_force_kernel(own, *all_refs):
    mid_ref, slope_ref, weight_ref, below_ref, above_ref = all_refs[:5]
    refs = dict(zip(SETS, all_refs[5:9]))
    point_refs = dict(zip(SETS, all_refs[9:13]))
    out_ref, left_ref = all_refs[13:15]
    pair_refs = dict(zip(SETS, all_refs[15:]))
    grid = Grid(own)
    m = grid.masks
    near = grid.cz + 2
    for which in SETS:
        for a, b, c in grid.cells_of(which, grid.inner):
            if which[0] == "g":
                weight = row_of(below_ref if b == 0 else above_ref, (a - 1) * near + c - 1)
            else:
                weight = row_of(weight_ref, grid.slope_row(a, b, c))
            put_pair(grid, (a, b, c), point_refs, pair_refs, weight)
    for place, (a, b, c) in enumerate(grid.own_targets()):
        tile = mid_ref[a, b - 1, c - 2]
        solute = tile[3:4] > 1.05
        left_ref[place] = target_block(
            grid.target(tile, a, b, c) * jnp.where(solute, 0.8, 0.6)
            + row_of(slope_ref, grid.slope_row(a, b, c)) * jnp.where(solute, 1.0 / 0.16, 1.0 / 0.09) * m[5]
            + jnp.where(solute, 1.3 / 0.16, 1.0 / 0.09) * m[6]
        )
        runs = grid.sources((a, b, c), SETS, grid.inner)
        add_force(left_ref, place, runs, refs, point_refs, pair_refs, nothing, store_four(out_ref, place))


def side_force_kernel(own, below_ref, above_ref, part_ref, edge_ref, point_ref, edge_point_ref, column_ref, left_ref, out_ref, pair_ref, edge_pair_ref):
    grid = Grid(own)
    refs = {"own": part_ref, "edge": edge_ref}
    point_refs = {"own": point_ref, "edge": edge_point_ref}
    pair_refs = {"own": pair_ref, "edge": edge_pair_ref}
    for which in refs:
        for a, b, c in grid.cells_of(which, grid.outer):
            weight = row_of(below_ref if a == 0 else above_ref, grid.slope_row(1, b, c))
            put_pair(grid, (a, b, c), point_refs, pair_refs, weight)
    for place, cell in enumerate(grid.own_targets()):
        runs = grid.sources(cell, tuple(refs), grid.outer)
        before, after = load_four(column_ref, place), store_four(out_ref, place)
        add_force(left_ref, place, runs, refs, point_refs, pair_refs, before, after)


def last_force_kernel(own, stage, mid_ref, below_ref, above_ref, ghost_ref, ghost_edge_ref, ghost_point_ref, ghost_edge_point_ref, column_ref, left_ref, vel_ref, *out_refs):
    new_vel_ref, new_loc_ref, pair_ref, edge_pair_ref = out_refs
    grid = Grid(own)
    near = grid.cz + 2
    refs = {"gown": ghost_ref, "gedge": ghost_edge_ref}
    point_refs = {"gown": ghost_point_ref, "gedge": ghost_edge_point_ref}
    pair_refs = {"gown": pair_ref, "gedge": edge_pair_ref}
    for which in refs:
        for a, b, c in grid.cells_of(which, grid.outer):
            weight = row_of(below_ref if b == 0 else above_ref, int(a > 0) * near + c - 1)
            put_pair(grid, (a, b, c), point_refs, pair_refs, weight)
    for place, (a, b, c) in enumerate(grid.own_targets()):
        parts = []
        runs = grid.sources((a, b, c), tuple(refs), grid.outer)
        after = lambda chunk, total: parts.append(total)
        add_force(left_ref, place, runs, refs, point_refs, pair_refs, load_four(column_ref, place), after)
        flat = [across(jnp.concatenate([part[k] for part in parts], axis=0)) for k in range(4)]
        row = slice(place, place + 1)
        tile = mid_ref[a, b - 1, c - 2]
        point, _ = grid.placed(tile, a, b, c)
        scale = tile[3:4]
        present = jnp.where(scale > 0.5, -2.0, 0.0)
        kick = half_kick * jnp.where(scale > 1.05, 1.6, 1.0)
        for axis in range(3):
            force = present * (flat[axis] - point[axis : axis + 1] * flat[3])
            speed = vel_ref[axis, row, :] + kick * force
            if stage == "middle":
                speed = speed + kick * force
            new_vel_ref[axis, row, :] = speed
            if stage == "last":
                new_loc_ref[axis, row, :] = tile[axis : axis + 1]
            else:
                new_loc_ref[place, axis : axis + 1, :] = tile[axis : axis + 1] + time_step * speed
        if stage != "last":
            new_loc_ref[place, 3:4, :] = scale


def on_device(positions, velocities, species, counts):
    cx, cy, cz, slots = positions.shape[1:]
    own = (cx, cy, cz)
    cells = cx * cy * cz
    ex, near = cx + 2, cz + 2
    vmem = pl.BlockSpec(memory_space=pltpu.VMEM)
    flat_shape = jax.ShapeDtypeStruct((3, cells, slots), jnp.float32)
    sizes = {"own": ex * cy * cz, "edge": ex * cy * 2, "gown": 2 * ex * cz, "gedge": 2 * ex * 2}

    def block(which):
        return jax.ShapeDtypeStruct((48, sizes[which] * slots), jnp.bfloat16)

    def points(which):
        return jax.ShapeDtypeStruct((8, sizes[which] * slots), jnp.float32)

    def sums(*count):
        return jax.ShapeDtypeStruct((*count, slots, slots), jnp.float32)

    def rows(count):
        return jax.ShapeDtypeStruct((count, slots), jnp.float32)

    def lefts(count):
        return jax.ShapeDtypeStruct((count, slots, 48), jnp.bfloat16)

    def call(kernel, operands, out_shape, pairs, scratch=()):
        return pl.pallas_call(
            kernel,
            out_shape=out_shape,
            in_specs=[vmem] * len(operands),
            out_specs=[vmem] * len(out_shape),
            scratch_shapes=[pltpu.VMEM(item.shape, item.dtype) for item in scratch],
            compiler_params=pltpu.CompilerParams(vmem_limit_bytes=GRANT),
            cost_estimate=pl.CostEstimate(
                flops=pairs * slots * slots * 50, bytes_accessed=pairs * slots * slots * 4, transcendentals=0
            ),
        )(*operands)

    pairs = {axis: lax.optimization_barrier(lax.axis_index(axis) % 2 == 0) for axis in ("gx", "gz")}

    rings = {"gx": None, "gz": None}

    def evaluate(location, velocity, stage, even):
        mid = ring_halo(location, "gx", 0, 1, even["gx"])
        mid_below, mid_above = neighbours(mid, "gy", 1, 1)
        low, high = neighbours(mid, "gz", 2, 2, even["gz"])
        inner, part, point, ghost, ghost_point, left = call(
            functools.partial(inner_density_kernel, own),
            [mid, mid_below, mid_above],
            [sums(cells), block("own"), points("own"), block("gown"), points("gown"), lefts(cells)],
            cells * 18,
        )
        tall, inner = lax.optimization_barrier((jnp.concatenate([low, high], axis=2), inner))
        below, above = neighbours(tall, "gy", 1, 1)
        own_sum, edge_sum, edge, edge_point, edge_left = call(
            functools.partial(outer_density_kernel, own),
            [low, high, inner, part, ghost, left],
            [sums(cells), sums(cx * cy * 2), block("edge"), points("edge"), lefts(cx * cy * 2)],
            cells * 27,
            [block("edge")],
        )
        slopes, weights, ghost_edge, ghost_edge_point = call(
            functools.partial(last_density_kernel, own),
            [mid, low, high, below, above, own_sum, edge_sum, left, edge_left],
            [rows(cx * cy * near), rows(cx * cy * near), block("gedge"), points("gedge")],
            cells * 9,
            [block("gedge")],
        )
        weights = weights.reshape(cx, cy, near, slots)
        side_below, side_above = neighbours(weights, "gx", 0, 1, even["gx"])
        weight_below, weight_above = neighbours(weights, "gy", 1, 1)
        column, left = call(
            functools.partial(column_force_kernel, own),
            [
                mid,
                slopes,
                weights.reshape(cx * cy * near, slots),
                weight_below.reshape(cx * near, slots),
                weight_above.reshape(cx * near, slots),
                *(part, edge, ghost, ghost_edge),
                *(point, edge_point, ghost_point, ghost_edge_point),
            ],
            [sums(4, cells), lefts(cells)],
            cells * 9,
            [block(which) for which in SETS],
        )
        sides, column = lax.optimization_barrier((jnp.concatenate([side_below, side_above], axis=0), column))
        corner_below, corner_above = neighbours(sides, "gy", 1, 1)
        (column,) = call(
            functools.partial(side_force_kernel, own),
            [
                side_below.reshape(cy * near, slots),
                side_above.reshape(cy * near, slots),
                *(part, edge, point, edge_point, column, left),
            ],
            [sums(4, cells)],
            cells * 12,
            [block("own"), block("edge")],
        )
        moved = flat_shape if stage == "last" else jax.ShapeDtypeStruct((cells, 4, slots), jnp.float32)
        return call(
            functools.partial(last_force_kernel, own, stage),
            [
                mid,
                corner_below.reshape(2 * near, slots),
                corner_above.reshape(2 * near, slots),
                *(ghost, ghost_edge, ghost_point, ghost_edge_point, column, left, velocity),
            ],
            [flat_shape, moved],
            cells * 6,
            [block("gown"), block("gedge")],
        )

    arrays = [pltpu.with_memory_space_constraint(x, pltpu.HBM) for x in (positions, velocities, species, counts)]
    location, velocity = pl.pallas_call(
        prepare_kernel,
        out_shape=[jax.ShapeDtypeStruct((cx, cy, cz, 4, slots), jnp.float32), flat_shape],
        in_specs=[pl.BlockSpec(memory_space=pltpu.HBM)] * 4,
        out_specs=[vmem] * 2,
        scratch_shapes=[pltpu.VMEM(array.shape, array.dtype) for array in arrays] + [pltpu.SemaphoreType.DMA((4,))],
        compiler_params=pltpu.CompilerParams(vmem_limit_bytes=GRANT),
        name="prepare",
    )(*arrays)
    for sweep, stage in enumerate(("first", "middle", "last")):
        velocity, moved = evaluate(location.reshape(cx, cy, cz, 4, slots), velocity, stage, pairs if sweep == 0 else rings)
        location = moved
    new_positions = moved
    return new_positions.reshape(positions.shape), velocity.reshape(positions.shape)


def solution(mesh):
    return jax.shard_map(
        on_device,
        mesh=mesh,
        in_specs=(
            P(None, "gx", "gy", "gz", None),
            P(None, "gx", "gy", "gz", None),
            P("gx", "gy", "gz", None),
            P("gx", "gy", "gz"),
        ),
        out_specs=(P(None, "gx", "gy", "gz", None), P(None, "gx", "gy", "gz", None)),
        check_vma=False,
    )
```

```python
import functools

import jax
import jax.numpy as jnp
from jax import lax
from jax.experimental import pallas as pl
from jax.experimental.pallas import tpu as pltpu
from jax.sharding import PartitionSpec as P


time_step = 0.05
half_kick = 0.5 * time_step
LANES = 128
GRANT = 8 * 1024 * 1024
ROOT = 1.3 ** (1.0 / 3.0)
STEPS = (-1, 0, 1)
SETS = ("own", "edge", "gown", "gedge")


def neighbours(cells, axis, dim, width, even=None):
    count = lax.axis_size(axis)
    size = cells.shape[dim]
    head = lax.slice_in_dim(cells, 0, width, axis=dim)
    tail = lax.slice_in_dim(cells, size - width, size, axis=dim)
    if count == 1:
        return tail, head
    if count == 2 and size == 2 * width:
        other = lax.ppermute(cells, axis, [(0, 1), (1, 0)])
        return (
            lax.slice_in_dim(other, width, size, axis=dim),
            lax.slice_in_dim(other, 0, width, axis=dim),
        )
    if even is None or count % 2:
        above = lax.ppermute(head, axis, [((i + 1) % count, i) for i in range(count)])
        below = lax.ppermute(tail, axis, [(i, (i + 1) % count) for i in range(count)])
        return below, above
    first, second = (cells, cells) if size == width else (jnp.where(even, tail, head), jnp.where(even, head, tail))
    second = lax.ppermute(second, axis, [(i, (i - 1 if i % 2 == 0 else i + 1) % count) for i in range(count)])
    first = lax.ppermute(first, axis, [(i, i ^ 1) for i in range(count)])
    return jnp.where(even, second, first), jnp.where(even, first, second)


def ring_halo(cells, axis, dim, width, even=None):
    below, above = neighbours(cells, axis, dim, width, even)
    return jnp.concatenate([below, cells, above], axis=dim)


def split3(value):
    high = value.astype(jnp.bfloat16).astype(jnp.float32)
    rest = value - high
    middle = rest.astype(jnp.bfloat16).astype(jnp.float32)
    return high, middle, rest - middle


def partner_block(row):
    high, middle, low = split3(row)
    first = jnp.concatenate([high, middle], axis=0).astype(jnp.bfloat16)
    last = jnp.concatenate([low, high], axis=0).astype(jnp.bfloat16)
    return jnp.concatenate([first, first, last], axis=0)


def target_block(row):
    high, middle, low = split3(row)
    stacked = jnp.concatenate([high, high, middle, middle, high, low], axis=0)
    return jnp.transpose(stacked).astype(jnp.bfloat16)


class Grid:
    def __init__(self, own):
        self.cx, self.cy, self.cz = own
        self.ex, self.ey, self.ez = own[0] + 2, own[1] + 2, own[2] + 4
        row = lax.broadcasted_iota(jnp.int32, (8, LANES), 0)
        self.row = row
        self.masks = [(row == k).astype(jnp.float32) for k in range(7)]
        self.spatial = self.masks[0] + self.masks[1] + self.masks[2]
        self.inner = range(1, self.cx + 1)
        self.outer = (0, self.ex - 1)

    def own_targets(self):
        return [(a, b, c) for a in self.inner for b in range(1, self.cy + 1) for c in range(2, self.cz + 2)]

    def edge_targets(self):
        return [(a, b, c) for a in self.inner for b in range(1, self.cy + 1) for c in (1, self.cz + 2)]

    def slope_row(self, a, b, c):
        return ((a - 1) * self.cy + b - 1) * (self.cz + 2) + c - 1

    def place(self, a, b, c):
        if c in (0, self.ez - 1):
            which, layer = "far", int(c > 0)
        elif c in (1, self.ez - 2):
            which, layer = "edge", int(c > 1)
        else:
            which, layer = "own", c - 2
        if 1 <= b <= self.cy:
            return which, (layer * self.ex + a) * self.cy + b - 1
        layers = self.cz if which == "own" else 2
        column = self.outer.index(a) if a in self.outer else a + 1
        return "g" + which, (int(b > 0) * layers + layer) * self.ex + column

    def cells_of(self, which, columns=None):
        columns = range(self.ex) if columns is None else columns
        rows = (0, self.ey - 1) if which[0] == "g" else range(1, self.cy + 1)
        layers = {"n": range(2, self.cz + 2), "e": (1, self.ez - 2), "r": (0, self.ez - 1)}[
            "n" if which.endswith("own") else "e" if which.endswith("edge") else "r"
        ]
        return [(a, b, c) for c in layers for a in columns for b in rows]

    def sources(self, target, sets, columns=None):
        found = {}
        for p in STEPS:
            for q in STEPS:
                for r in STEPS:
                    a, b, c = target[0] + p, target[1] + q, target[2] + r
                    which, index = self.place(a, b, c)
                    if which in sets and (columns is None or a in columns):
                        found.setdefault(which, []).append((index, p == q == r == 0))
        runs = []
        for which in sets:
            entries = sorted(found.get(which, []))
            while entries:
                length = 1
                while length < len(entries) and entries[length][0] == entries[0][0] + length:
                    length += 1
                count = min(length, 2 if length % 2 == 0 else 3)
                same = [k for k in range(count) if entries[k][1]]
                runs.append((which, entries[0][0], count, same[0] if same else -1))
                entries = entries[count:]
        return runs

    def placed(self, tile, a, b, c):
        m = self.masks
        shift = (
            (a + 0.5 - 0.5 * self.ex) * m[0]
            + (b + 0.5 - 0.5 * self.ey) * m[1]
            + (m[4] + (c + 0.5 - 0.5 * self.ez) * m[2])
        )
        point = jnp.concatenate([tile, jnp.zeros((4, LANES), jnp.float32)], axis=0)
        point = point * self.spatial + shift
        return point, jnp.sum(point * point, axis=0, keepdims=True)

    def put_partner(self, tile, cell, refs, point_refs=None):
        which, index = self.place(*cell)
        lanes = slice(index * LANES, (index + 1) * LANES)
        point, bulk = self.placed(tile, *cell)
        scale = tile[3:4]
        refs[which][:, lanes] = partner_block(jnp.where(self.row == 3, 1.0 - bulk, point) * scale)
        if point_refs is not None:
            strength = jnp.where(scale > 1.05, 0.4 / ROOT, 0.3)
            point_refs[which][:, lanes] = jnp.where(
                self.row == 3, strength, jnp.where(self.row == 4, scale, point)
            )

    def target(self, tile, a, b, c):
        point, bulk = self.placed(tile, a, b, c)
        twice = jnp.where(self.row == 4, 2.0 - bulk, 2.0 * point)
        return twice + self.masks[3]


def across(total):
    return jnp.sum(jnp.transpose(total), axis=0, keepdims=True)


def add_density(left_ref, place, runs, refs, before, after):
    rows = 128
    for start in range(0, LANES, rows):
        chunk = slice(start, start + rows)
        total = before(chunk)
        for which, first, count, same in runs:
            near = jnp.dot(
                left_ref[place, chunk, :],
                refs[which][:, first * LANES : (first + count) * LANES],
                preferred_element_type=jnp.float32,
            )
            for k in range(count):
                part = jnp.maximum(near[:, k * LANES : (k + 1) * LANES], 0.0)
                if k == same:
                    i = lax.broadcasted_iota(jnp.int32, (rows, LANES), 0)
                    j = lax.broadcasted_iota(jnp.int32, (rows, LANES), 1)
                    part = jnp.where(i + start == j, 0.0, part)
                cube = part * part * part
                total = cube if total is None else total + cube
        after(chunk, total)


def store_to(ref, place):
    def after(chunk, total):
        ref[place, chunk, :] = total

    return after


def nothing(chunk):
    return None


def prepare_kernel(pos_hbm, vel_hbm, species_hbm, counts_hbm, loc_ref, out_ref, pos_ref, vel_ref, species_ref, counts_ref, arrived):
    copies = [
        pltpu.make_async_copy(source, target, arrived.at[k])
        for k, (source, target) in enumerate(
            ((pos_hbm, pos_ref), (vel_hbm, vel_ref), (species_hbm, species_ref), (counts_hbm, counts_ref))
        )
    ]
    for copy in copies:
        copy.start()
    for copy in copies:
        copy.wait()
    cx, cy, cz = pos_ref.shape[1:4]
    slot = lax.broadcasted_iota(jnp.int32, (1, LANES), 1)
    for a in range(cx):
        for b in range(cy):
            for c in range(cz):
                place = (a * cy + b) * cz + c
                one = slice(c, c + 1)
                for axis in range(3):
                    loc_ref[a, b, c, axis : axis + 1, :] = pos_ref[axis, a, b, one, :]
                    out_ref[axis, place : place + 1, :] = vel_ref[axis, a, b, one, :]
                kind = jnp.where(species_ref[a, b, one, :] == 1, ROOT, 1.0)
                count = jnp.broadcast_to(counts_ref[a, b : b + 1, one], (1, LANES))
                loc_ref[a, b, c, 3:4, :] = jnp.where(slot < count, kind, 0.0)


def inner_density_kernel(own, mid_ref, below_ref, above_ref, sum_ref, part_ref, point_ref, ghost_ref, ghost_point_ref, left_ref):
    grid = Grid(own)
    refs = {"own": part_ref, "gown": ghost_ref}
    point_refs = {"own": point_ref, "gown": ghost_point_ref}
    for a, b, c in grid.cells_of("own"):
        grid.put_partner(mid_ref[a, b - 1, c - 2], (a, b, c), refs, point_refs)
    for a, b, c in grid.cells_of("gown"):
        tile = (below_ref if b == 0 else above_ref)[a, 0, c - 2]
        grid.put_partner(tile, (a, b, c), refs, point_refs)
    for place, (a, b, c) in enumerate(grid.own_targets()):
        left_ref[place] = target_block(grid.target(mid_ref[a, b - 1, c - 2], a, b, c))
        runs = grid.sources((a, b, c), ("own", "gown"))
        add_density(left_ref, place, runs, refs, nothing, store_to(sum_ref, place))


def outer_density_kernel(own, low_ref, high_ref, inner_ref, part_ref, ghost_ref, left_ref, own_sum_ref, edge_sum_ref, edge_ref, edge_point_ref, edge_left_ref, far_ref):
    grid = Grid(own)
    refs = {"own": part_ref, "gown": ghost_ref, "edge": edge_ref, "far": far_ref}

    def tile_of(a, b, c):
        return low_ref[a, b - 1, c] if c < 2 else high_ref[a, b - 1, c - grid.cz - 2]

    for cell in grid.cells_of("edge"):
        grid.put_partner(tile_of(*cell), cell, refs, {"edge": edge_point_ref})
    for cell in grid.cells_of("far"):
        grid.put_partner(tile_of(*cell), cell, refs)
    for place, cell in enumerate(grid.edge_targets()):
        edge_left_ref[place] = target_block(grid.target(tile_of(*cell), *cell))
        runs = grid.sources(cell, ("own", "gown", "edge", "far"))
        add_density(edge_left_ref, place, runs, refs, nothing, store_to(edge_sum_ref, place))
    for place, cell in enumerate(grid.own_targets()):
        runs = grid.sources(cell, ("edge",))
        before = lambda chunk, place=place: inner_ref[place, chunk, :]
        add_density(left_ref, place, runs, refs, before, store_to(own_sum_ref, place))


def last_density_kernel(own, mid_ref, low_ref, high_ref, below_ref, above_ref, own_sum_ref, edge_sum_ref, left_ref, edge_left_ref, slope_ref, weight_ref, ghost_ref, ghost_point_ref, far_ref):
    grid = Grid(own)
    refs = {"gedge": ghost_ref, "gfar": far_ref}
    for which in ("gedge", "gfar"):
        for a, b, c in grid.cells_of(which):
            tile = (below_ref if b == 0 else above_ref)[a, 0, c if c < 2 else c - grid.cz]
            grid.put_partner(tile, (a, b, c), refs, {"gedge": ghost_point_ref} if which == "gedge" else None)
    groups = ((grid.own_targets(), own_sum_ref, left_ref), (grid.edge_targets(), edge_sum_ref, edge_left_ref))
    for targets, sum_ref, rows_ref in groups:
        for place, (a, b, c) in enumerate(targets):
            if c < 2:
                tile = low_ref[a, b - 1, c]
            elif c >= grid.cz + 2:
                tile = high_ref[a, b - 1, c - grid.cz - 2]
            else:
                tile = mid_ref[a, b - 1, c - 2]
            runs = grid.sources((a, b, c), ("gedge", "gfar"))
            parts = []
            before = lambda chunk, place=place, sum_ref=sum_ref: sum_ref[place, chunk, :]
            add_density(rows_ref, place, runs, refs, before, lambda chunk, total: parts.append(total))
            density = across(jnp.concatenate(parts, axis=0))
            scale = tile[3:4]
            slope = jnp.where(scale > 0.5, -0.5, 0.0) / jnp.sqrt(density + 1.0)
            where = grid.slope_row(a, b, c)
            slope_ref[where : where + 1, :] = slope
            weight_ref[where : where + 1, :] = slope * jnp.where(scale > 1.05, 0.75 / (ROOT * ROOT), 0.75)


def put_pair(grid, cell, point_refs, pair_refs, weight):
    which, index = grid.place(*cell)
    lanes = slice(index * LANES, (index + 1) * LANES)
    scale = point_refs[which][4:5, lanes]
    row = jnp.where(grid.row == 5, 0.75 * scale, jnp.where(grid.row == 6, weight, 0.0))
    high = row.astype(jnp.bfloat16).astype(jnp.float32)
    first = jnp.concatenate([high, row - high], axis=0).astype(jnp.bfloat16)
    last = jnp.concatenate([jnp.zeros((8, LANES), jnp.float32), high], axis=0).astype(jnp.bfloat16)
    pair_refs[which][:, lanes] = jnp.concatenate([first, first, last], axis=0)


def add_force(left_ref, place, runs, refs, point_refs, pair_refs, before, after):
    rows = 128
    for start in range(0, LANES, rows):
        chunk = slice(start, start + rows)
        total = before(chunk)
        left = left_ref[place, chunk, :]
        for which, first, count, _ in runs:
            span = slice(first * LANES, (first + count) * LANES)
            near = jnp.dot(left, refs[which][:, span], preferred_element_type=jnp.float32)
            kappa = jnp.dot(left, pair_refs[which][:, span], preferred_element_type=jnp.float32)
            value_ref = point_refs[which]
            for k in range(count):
                part = slice(k * LANES, (k + 1) * LANES)
                lanes = slice((first + k) * LANES, (first + k + 1) * LANES)
                s = jnp.maximum(near[:, part], 0.0)
                w = s * (value_ref[3:4, lanes] + s * kappa[:, part])
                new = [w * value_ref[axis : axis + 1, lanes] for axis in range(3)] + [w]
                total = new if total is None else [old + more for old, more in zip(total, new)]
        after(chunk, total)


def store_four(ref, place):
    def after(chunk, total):
        for k in range(4):
            ref[k, place, chunk, :] = total[k]

    return after


def load_four(ref, place):
    def before(chunk):
        return [ref[k, place, chunk, :] for k in range(4)]

    return before


def row_of(ref, index):
    return ref[index : index + 1, :]


def column_force_kernel(own, *all_refs):
    mid_ref, slope_ref, weight_ref, below_ref, above_ref = all_refs[:5]
    refs = dict(zip(SETS, all_refs[5:9]))
    point_refs = dict(zip(SETS, all_refs[9:13]))
    out_ref, left_ref = all_refs[13:15]
    pair_refs = dict(zip(SETS, all_refs[15:]))
    grid = Grid(own)
    m = grid.masks
    near = grid.cz + 2
    for which in SETS:
        for a, b, c in grid.cells_of(which, grid.inner):
            if which[0] == "g":
                weight = row_of(below_ref if b == 0 else above_ref, (a - 1) * near + c - 1)
            else:
                weight = row_of(weight_ref, grid.slope_row(a, b, c))
            put_pair(grid, (a, b, c), point_refs, pair_refs, weight)
    for place, (a, b, c) in enumerate(grid.own_targets()):
        tile = mid_ref[a, b - 1, c - 2]
        solute = tile[3:4] > 1.05
        left_ref[place] = target_block(
            grid.target(tile, a, b, c) * jnp.where(solute, 0.8, 0.6)
            + row_of(slope_ref, grid.slope_row(a, b, c)) * jnp.where(solute, 1.0 / 0.16, 1.0 / 0.09) * m[5]
            + jnp.where(solute, 1.3 / 0.16, 1.0 / 0.09) * m[6]
        )
        runs = grid.sources((a, b, c), SETS, grid.inner)
        add_force(left_ref, place, runs, refs, point_refs, pair_refs, nothing, store_four(out_ref, place))


def side_force_kernel(own, below_ref, above_ref, part_ref, edge_ref, point_ref, edge_point_ref, column_ref, left_ref, out_ref, pair_ref, edge_pair_ref):
    grid = Grid(own)
    refs = {"own": part_ref, "edge": edge_ref}
    point_refs = {"own": point_ref, "edge": edge_point_ref}
    pair_refs = {"own": pair_ref, "edge": edge_pair_ref}
    for which in refs:
        for a, b, c in grid.cells_of(which, grid.outer):
            weight = row_of(below_ref if a == 0 else above_ref, grid.slope_row(1, b, c))
            put_pair(grid, (a, b, c), point_refs, pair_refs, weight)
    for place, cell in enumerate(grid.own_targets()):
        runs = grid.sources(cell, tuple(refs), grid.outer)
        before, after = load_four(column_ref, place), store_four(out_ref, place)
        add_force(left_ref, place, runs, refs, point_refs, pair_refs, before, after)


def last_force_kernel(own, stage, mid_ref, below_ref, above_ref, ghost_ref, ghost_edge_ref, ghost_point_ref, ghost_edge_point_ref, column_ref, left_ref, vel_ref, *out_refs):
    new_vel_ref, new_loc_ref, pair_ref, edge_pair_ref = out_refs
    grid = Grid(own)
    near = grid.cz + 2
    refs = {"gown": ghost_ref, "gedge": ghost_edge_ref}
    point_refs = {"gown": ghost_point_ref, "gedge": ghost_edge_point_ref}
    pair_refs = {"gown": pair_ref, "gedge": edge_pair_ref}
    for which in refs:
        for a, b, c in grid.cells_of(which, grid.outer):
            weight = row_of(below_ref if b == 0 else above_ref, int(a > 0) * near + c - 1)
            put_pair(grid, (a, b, c), point_refs, pair_refs, weight)
    for place, (a, b, c) in enumerate(grid.own_targets()):
        parts = []
        runs = grid.sources((a, b, c), tuple(refs), grid.outer)
        after = lambda chunk, total: parts.append(total)
        add_force(left_ref, place, runs, refs, point_refs, pair_refs, load_four(column_ref, place), after)
        flat = [across(jnp.concatenate([part[k] for part in parts], axis=0)) for k in range(4)]
        row = slice(place, place + 1)
        tile = mid_ref[a, b - 1, c - 2]
        point, _ = grid.placed(tile, a, b, c)
        scale = tile[3:4]
        present = jnp.where(scale > 0.5, -2.0, 0.0)
        kick = half_kick * jnp.where(scale > 1.05, 1.6, 1.0)
        for axis in range(3):
            force = present * (flat[axis] - point[axis : axis + 1] * flat[3])
            speed = vel_ref[axis, row, :] + kick * force
            if stage == "middle":
                speed = speed + kick * force
            new_vel_ref[axis, row, :] = speed
            if stage == "last":
                new_loc_ref[axis, row, :] = tile[axis : axis + 1]
            else:
                new_loc_ref[place, axis : axis + 1, :] = tile[axis : axis + 1] + time_step * speed
        if stage != "last":
            new_loc_ref[place, 3:4, :] = scale


def on_device(positions, velocities, species, counts):
    cx, cy, cz, slots = positions.shape[1:]
    own = (cx, cy, cz)
    cells = cx * cy * cz
    ex, near = cx + 2, cz + 2
    vmem = pl.BlockSpec(memory_space=pltpu.VMEM)
    flat_shape = jax.ShapeDtypeStruct((3, cells, slots), jnp.float32)
    sizes = {"own": ex * cy * cz, "edge": ex * cy * 2, "gown": 2 * ex * cz, "gedge": 2 * ex * 2}

    def block(which):
        return jax.ShapeDtypeStruct((48, sizes[which] * slots), jnp.bfloat16)

    def points(which):
        return jax.ShapeDtypeStruct((8, sizes[which] * slots), jnp.float32)

    def sums(*count):
        return jax.ShapeDtypeStruct((*count, slots, slots), jnp.float32)

    def rows(count):
        return jax.ShapeDtypeStruct((count, slots), jnp.float32)

    def lefts(count):
        return jax.ShapeDtypeStruct((count, slots, 48), jnp.bfloat16)

    def call(kernel, operands, out_shape, pairs, scratch=()):
        return pl.pallas_call(
            kernel,
            out_shape=out_shape,
            in_specs=[vmem] * len(operands),
            out_specs=[vmem] * len(out_shape),
            scratch_shapes=[pltpu.VMEM(item.shape, item.dtype) for item in scratch],
            compiler_params=pltpu.CompilerParams(vmem_limit_bytes=GRANT),
            cost_estimate=pl.CostEstimate(
                flops=pairs * slots * slots * 50, bytes_accessed=pairs * slots * slots * 4, transcendentals=0
            ),
        )(*operands)

    even = lax.optimization_barrier(lax.axis_index("gz") % 2 == 0)

    def evaluate(location, velocity, stage):
        mid = ring_halo(location, "gx", 0, 1)
        mid_below, mid_above = neighbours(mid, "gy", 1, 1)
        low, high = neighbours(mid, "gz", 2, 2, even)
        inner, part, point, ghost, ghost_point, left = call(
            functools.partial(inner_density_kernel, own),
            [mid, mid_below, mid_above],
            [sums(cells), block("own"), points("own"), block("gown"), points("gown"), lefts(cells)],
            cells * 18,
        )
        tall, inner = lax.optimization_barrier((jnp.concatenate([low, high], axis=2), inner))
        below, above = neighbours(tall, "gy", 1, 1)
        own_sum, edge_sum, edge, edge_point, edge_left = call(
            functools.partial(outer_density_kernel, own),
            [low, high, inner, part, ghost, left],
            [sums(cells), sums(cx * cy * 2), block("edge"), points("edge"), lefts(cx * cy * 2)],
            cells * 27,
            [block("edge")],
        )
        slopes, weights, ghost_edge, ghost_edge_point = call(
            functools.partial(last_density_kernel, own),
            [mid, low, high, below, above, own_sum, edge_sum, left, edge_left],
            [rows(cx * cy * near), rows(cx * cy * near), block("gedge"), points("gedge")],
            cells * 9,
            [block("gedge")],
        )
        weights = weights.reshape(cx, cy, near, slots)
        side_below, side_above = neighbours(weights, "gx", 0, 1)
        weight_below, weight_above = neighbours(weights, "gy", 1, 1)
        column, left = call(
            functools.partial(column_force_kernel, own),
            [
                mid,
                slopes,
                weights.reshape(cx * cy * near, slots),
                weight_below.reshape(cx * near, slots),
                weight_above.reshape(cx * near, slots),
                *(part, edge, ghost, ghost_edge),
                *(point, edge_point, ghost_point, ghost_edge_point),
            ],
            [sums(4, cells), lefts(cells)],
            cells * 9,
            [block(which) for which in SETS],
        )
        sides, column = lax.optimization_barrier((jnp.concatenate([side_below, side_above], axis=0), column))
        corner_below, corner_above = neighbours(sides, "gy", 1, 1)
        (column,) = call(
            functools.partial(side_force_kernel, own),
            [
                side_below.reshape(cy * near, slots),
                side_above.reshape(cy * near, slots),
                *(part, edge, point, edge_point, column, left),
            ],
            [sums(4, cells)],
            cells * 12,
            [block("own"), block("edge")],
        )
        moved = flat_shape if stage == "last" else jax.ShapeDtypeStruct((cells, 4, slots), jnp.float32)
        return call(
            functools.partial(last_force_kernel, own, stage),
            [
                mid,
                corner_below.reshape(2 * near, slots),
                corner_above.reshape(2 * near, slots),
                *(ghost, ghost_edge, ghost_point, ghost_edge_point, column, left, velocity),
            ],
            [flat_shape, moved],
            cells * 6,
            [block("gown"), block("gedge")],
        )

    arrays = [pltpu.with_memory_space_constraint(x, pltpu.HBM) for x in (positions, velocities, species, counts)]
    location, velocity = pl.pallas_call(
        prepare_kernel,
        out_shape=[jax.ShapeDtypeStruct((cx, cy, cz, 4, slots), jnp.float32), flat_shape],
        in_specs=[pl.BlockSpec(memory_space=pltpu.HBM)] * 4,
        out_specs=[vmem] * 2,
        scratch_shapes=[pltpu.VMEM(array.shape, array.dtype) for array in arrays] + [pltpu.SemaphoreType.DMA((4,))],
        compiler_params=pltpu.CompilerParams(vmem_limit_bytes=GRANT),
        name="prepare",
    )(*arrays)
    for stage in ("first", "middle", "last"):
        velocity, moved = evaluate(location.reshape(cx, cy, cz, 4, slots), velocity, stage)
        location = moved
    new_positions = moved
    return new_positions.reshape(positions.shape), velocity.reshape(positions.shape)


def solution(mesh):
    return jax.shard_map(
        on_device,
        mesh=mesh,
        in_specs=(
            P(None, "gx", "gy", "gz", None),
            P(None, "gx", "gy", "gz", None),
            P("gx", "gy", "gz", None),
            P("gx", "gy", "gz"),
        ),
        out_specs=(P(None, "gx", "gy", "gz", None), P(None, "gx", "gy", "gz", None)),
        check_vma=False,
    )
```
